256 devices in a mesh: dp: 8 (over z_lo, x), ctx: 32 (over y, z_hi, core).
Axes of the slice: x: 4, y: 4, z: 8 (z_hi: 4, z_lo: 2; z = z_hi * 2 + z_lo), core: 2. Of those that a mesh axis runs over, the one named last changes fastest.
Arguments:
- grad_out: bfloat16 [8, 4096, 2048], P('dp', 'ctx'), may hold values from -6 to 6
- saved_input: bfloat16 [8, 4096, 2048], P('dp', 'ctx'), may hold values from -6 to 6
- gate_value: bfloat16 [8, 4096, 2048], P('dp', 'ctx'), may hold values from -6 to 6
- filter_taps: bfloat16 [2048, 4096], P(None, 'ctx'), may hold values from -0.09375 to 0.09375
- skip_gain: float32 [2048], replicated, may hold values from 0.1 to 1.9
- lang_ids: int32 [8, 4096], P('dp', 'ctx'), may hold values from 0 to 15
- doc_ids: int32 [8, 4096], P('dp', 'ctx'), may hold values from 0 to 31, never falling along the last dimension, each value on 1 to 1024 neighbouring positions
- dro_weight: float32 [16], replicated, may hold values from 0.25 to 4
Outputs:
- d_input: bfloat16 [8, 4096, 2048], P('dp', 'ctx')
- d_gate: bfloat16 [8, 4096, 2048], P('dp', 'ctx')
- d_filter: float32 [2048, 4096], P('ctx', 'dp')
The draws below stay inside these ranges and needn't reach their ends.
Inputs may be any that keep to these rules, and one draw needn't show every extreme that they name: `doc_ids`: in each sequence the document numbers never fall, and every number from 0 to 31 occurs.
All inputs are finite; a program needn't handle non-finite values.
Results may differ from the reference program's by a relative error of at most 0.017.
Values may be sent and summed in bfloat16 or wider, within the bound.
A program may use at most 128 MiB of HBM per device.

```python
import math
import jax
import jax.numpy as jnp
import numpy as np
from jax import lax

C = 2048
T_DEV = 128
GROUPS = 16
NDOCS = 32
BATCH = 8
SEQ = 4096
N_CTX = 32


def plant(drawn, rng, low, high):
    place = [jax.random.randint(jax.random.fold_in(rng, axis), (), 0, length) for axis, length in enumerate(drawn.shape)]
    widest = drawn.shape.index(max(drawn.shape))
    beside = place[:widest] + [(place[widest] + 1) % drawn.shape[widest]] + place[widest + 1:]
    return drawn.at[tuple(place)].set(low).at[tuple(beside)].set(high)


def steps_of(own_key, shape, split, smallest, largest):
    factor_of = 1.0
    for axis_at, parts in split:
        steps = jax.random.uniform(jax.random.fold_in(jax.random.fold_in(own_key, 6), axis_at), (parts,), jnp.float32, smallest / len(split), largest / len(split))
        factor_of = factor_of * jnp.repeat(jnp.exp(steps), shape[axis_at] // parts).reshape((-1,) + (1,) * (len(shape) - 1 - axis_at))
    return factor_of


def split_up(count, total, limit, lean):
    weights = [(1 << 20) // math.isqrt(grade ** lean) + 1 for grade in range(2, count + 1)]
    rest, given = total - limit - (count - 1), [1] * (count - 1)
    while rest > 0:
        movable = [i for i in range(count - 1) if given[i] < limit]
        mass, budget = sum([weights[i] for i in movable]), rest
        for i in movable:
            addition = min(limit - given[i], max(1, budget * weights[i] // mass), rest)
            given[i] = given[i] + addition
            rest = rest - addition
    return np.array([limit] + given)


def uneven_parts(rng, amount, total, most, slope):
    if amount == 2:
        one = jax.random.randint(rng, (), max(1, total - most), min(most, total - 1) + 1)
        return jnp.stack([one, total - one])
    tallies = jnp.asarray(split_up(amount, total, most, slope), jnp.int32)
    couples = (amount - 1) // 2
    donor, sink = tallies[1:1 + 2 * couples:2], tallies[2:2 + 2 * couples:2]
    slack = jnp.minimum(donor - 1, most - sink)
    shifted = jax.random.randint(jax.random.fold_in(rng, 1), (couples,), 0, 1 << 20) % (slack + 1)
    tallies = tallies.at[1:1 + 2 * couples:2].set(donor - shifted).at[2:2 + 2 * couples:2].set(sink + shifted)
    return tallies[jax.random.permutation(jax.random.fold_in(rng, 2), amount)]


def gaussian(key, extent, deviation, most, shards=(), held_as=jnp.bfloat16):
    array = deviation * jax.random.normal(key, extent, jnp.float32)
    if shards:
        array = array * steps_of(key, extent, shards, -0.22, 0.18)
    return jnp.clip(array, -most, most).astype(held_as)


def setup_inputs(seed: int = 0) -> dict:
    key_of = jax.random.split(jax.random.key(seed), 9)
    return {
        "grad_out": gaussian(key_of[0], (BATCH, SEQ, C), 1.0, 6.0, ((0, 8), (1, 32))),
        "saved_input": gaussian(key_of[1], (BATCH, SEQ, C), 1.0, 6.0, ((0, 8), (1, 32))),
        "gate_value": gaussian(key_of[2], (BATCH, SEQ, C), 1.0, 6.0, ((0, 8), (1, 32))),
        "filter_taps": gaussian(key_of[3], (C, SEQ), (T_DEV * N_CTX) ** -0.5, 0.09375, ((1, 32),)),
        "skip_gain": jnp.clip(1.0 + 0.18 * jax.random.normal(key_of[4], (C,), jnp.float32), 0.1, 1.9),
        "lang_ids": plant(jax.random.randint(key_of[5], (BATCH, SEQ), 0, GROUPS), jax.random.fold_in(key_of[5], 1), 0, GROUPS - 1).astype(jnp.int32),
        "doc_ids": jax.vmap(lambda own: jnp.searchsorted(jnp.cumsum(uneven_parts(own, NDOCS, SEQ, T_DEV * N_CTX // 4, 1)), jnp.arange(SEQ), side="right"))(jax.random.split(key_of[6], BATCH)).reshape((BATCH, SEQ)).astype(jnp.int32),
        "dro_weight": jnp.clip(jnp.exp(jax.random.uniform(key_of[7], (GROUPS,), jnp.float32, math.log(0.25), math.log(4.0))), 0.25, 4.0),
    }


def reference(grad_out, saved_input, gate_value, filter_taps, skip_gain, lang_ids, doc_ids, dro_weight):
    length = grad_out.shape[1]
    width = grad_out.shape[2]
    size = 2 * length
    lang_hot = lang_ids[..., None] == jnp.arange(GROUPS, dtype=jnp.int32)
    group_weight = jnp.sum(jnp.where(lang_hot, dro_weight, jnp.zeros_like(dro_weight)), axis=-1)
    doc_hot = (doc_ids[..., None] == jnp.arange(NDOCS, dtype=jnp.int32)).astype(jnp.float32)
    counts = jnp.sum(doc_hot, axis=1)
    doc_len = jnp.sum(doc_hot * counts[:, None, :], axis=-1)
    mean_len = length / NDOCS
    scale = group_weight * (2.0 * mean_len) / (doc_len + mean_len)
    grad_scaled = grad_out.astype(jnp.float32) * scale[..., None]
    grad_conv = (grad_scaled * gate_value.astype(jnp.float32)).astype(jnp.bfloat16)
    filt = jnp.fft.fft(filter_taps.astype(jnp.float32), n=size, axis=1)
    skip = skip_gain[:, None]

    def one(total, items):
        signal, grad = items
        sig = signal.astype(jnp.float32).T
        grd = grad.astype(jnp.float32).T
        sig_s = jnp.fft.fft(sig, n=size, axis=1)
        grd_s = jnp.fft.fft(grd, n=size, axis=1)
        mixed = (jnp.real(jnp.fft.ifft(filt * sig_s, axis=1))[:, :length] + skip * sig).astype(jnp.bfloat16)
        back = (jnp.real(jnp.fft.ifft(jnp.conj(filt) * grd_s, axis=1))[:, :length] + skip * grd).astype(jnp.bfloat16)
        lagged = jnp.real(jnp.fft.ifft(jnp.conj(sig_s) * grd_s, axis=1))[:, :length]
        return total + lagged, (mixed.T, back.T)

    total, outputs = lax.scan(one, jnp.zeros((width, length), jnp.float32), (saved_input, grad_conv))
    mixed_all, back_all = outputs
    d_gate = (grad_scaled * mixed_all.astype(jnp.float32)).astype(jnp.bfloat16)
    return back_all, d_gate, total
```

```python
import functools
import math

import jax
import jax.numpy as jnp
import numpy as np
from jax import lax
from jax.experimental import pallas as pl
from jax.experimental.pallas import tpu as pltpu
from jax.sharding import PartitionSpec as P

MESH = pl.DeviceIdType.MESH
BF = jnp.bfloat16
F32 = jnp.float32
NCTX, NDP, NX = 32, 8, 4
LEN = 4096
GR = 8
CH1, CH2 = 4, 8


def tables():
    k1 = np.arange(32)
    a = np.arange(32)
    b = np.arange(128)
    phi = 2 * math.pi / 128 * ((a[None, :] * (4 * k1[:, None] + 1)) % 128)
    first = np.zeros((64, 128), np.float32)
    first[:, :32] = np.stack([np.cos(phi), -np.sin(phi)], 1).reshape(64, 32)
    last = np.zeros((32, 128), np.float32)
    last[:, :64] = first[:, :32].T / LEN
    alpha = 2 * math.pi / 16384 * ((b[None, :] * (4 * k1[:, None] + 1)) % 16384)
    beta = 2 * math.pi / 128 * ((b[None, :] * b[:, None]) % 128)
    f = lambda v: jnp.asarray(v.astype(np.float32))
    return (
        jnp.asarray(first, BF),
        jnp.asarray(last, BF),
        f(np.cos(alpha)),
        f(np.sin(alpha)),
        f(np.cos(beta)),
        f(np.sin(beta)),
    )


def iota(shape, dim):
    return lax.broadcasted_iota(jnp.int32, shape, dim)


def swap(x):
    return pltpu.roll(x, 64, axis=1)


def kernel(
    grad, sig, gate, taps, skip, lang, docs, dro, first, last, cosa, sina, cosb, sinb,
    d_input, d_gate, d_filter,
    docs_out, docs_all, hall, htime, scale, mats, matst, fone, ftwo, send1, recv1, send2, recv2,
    ybuf, vbuf, qbuf, hspec, xspec, dfs, dfr,
    doc_s, doc_r, tap_s, tap_r, gat_s, gat_r, one_s, one_r, two_s, two_r, df_s, df_r, own,
):
    me = lax.axis_index("ctx")
    dp = lax.axis_index("dp")
    xs = lax.rem(dp, NX)
    zl = dp // NX
    low = iota((16, 128), 1) < 64

    def peer_of(p):
        return lax.rem(me + p, NCTX)

    def dp_of(q):
        return lax.rem(dp + q, NDP)

    def x_of(q):
        return zl * NX + lax.rem(xs + q, NX)

    barrier = pltpu.get_barrier_semaphore()

    @pl.loop(1, NCTX)
    def _(p):
        pl.semaphore_signal(barrier, inc=1, device_id={"ctx": peer_of(p)}, device_id_type=MESH)

    @pl.loop(1, NDP)
    def _(q):
        pl.semaphore_signal(barrier, inc=1, device_id={"dp": dp_of(q)}, device_id_type=MESH)

    docs_row = docs[...]
    docs_out[...] = jnp.broadcast_to(docs_row, (8, 128))
    docs_all[me] = jnp.broadcast_to(docs_row, (8, 128))
    pl.semaphore_wait(barrier, NCTX - 1 + NDP - 1)

    @pl.loop(1, NCTX)
    def _(p):
        peer = peer_of(p)
        pltpu.make_async_remote_copy(
            docs_out, docs_all.at[me], doc_s, doc_r, device_id={"ctx": peer}, device_id_type=MESH
        ).start()

    def tap_rows(j):
        return taps.at[pl.ds(pl.multiple_of(64 * j + 16 * xs, 16), 16), :]

    @pl.loop(1, NCTX)
    def _(p):
        peer = peer_of(p)
        pltpu.make_async_remote_copy(
            tap_rows(peer), hall.at[xs, me], tap_s, tap_r, device_id={"ctx": peer}, device_id_type=MESH
        ).start()

    own_taps = pltpu.make_async_copy(tap_rows(me), hall.at[xs, me], own.at[0])
    own_taps.start()

    def column(row):
        return jnp.broadcast_to(row.astype(F32), (128, 128)).T

    own_docs = column(docs_row)
    own_lang = column(lang[...])
    weight = jnp.zeros((128, 128), F32)
    for group in range(16):
        weight = jnp.where(own_lang == float(group), dro[group], weight)
    pltpu.make_async_copy(docs_all.at[0:31], docs_all.at[0:31], doc_r).wait()

    def count(a, total):
        row = jnp.broadcast_to(docs_all[a][0:1].astype(F32), (128, 128))
        return total + jnp.where(row == own_docs, 1.0, 0.0)

    hits = lax.fori_loop(0, NCTX, count, jnp.zeros((128, 128), F32))
    doc_len = jnp.sum(hits, axis=1, keepdims=True)
    scale[...] = weight * 256.0 / (doc_len + 128.0)

    for m in range(16):
        cols = slice(128 * m, 128 * m + 128)

        @pl.loop(0, GR)
        def _(g):
            rows = pl.ds(pl.multiple_of(16 * g, 16), 16)
            u = sig[0, rows, cols].astype(F32)
            dy = grad[0, rows, cols].astype(F32) * scale[rows, :]
            dz = dy * gate[0, rows, cols].astype(F32)
            send1[g, 2 * m] = jnp.where(low, u, swap(dz)).astype(BF)
            send1[g, 2 * m + 1] = jnp.where(low, swap(u), dz).astype(BF)

    per1 = GR // CH1

    def send_in(ch):
        span = slice(per1 * ch, per1 * ch + per1)

        @pl.loop(1, NCTX)
        def _(p):
            peer = peer_of(p)
            pltpu.make_async_remote_copy(
                send1.at[span, peer], recv1.at[span, me], one_s.at[ch], one_r.at[ch],
                device_id={"ctx": peer}, device_id_type=MESH,
            ).start()

    own_one = pltpu.make_async_copy(send1.at[:, me], recv1.at[:, me], own.at[1])
    own_one.start()
    send_in(0)
    own_taps.wait()
    pltpu.make_async_copy(hall.at[0, 0:31], hall.at[0, 0:31], tap_r).wait()

    @pl.loop(1, NX)
    def _(q):
        pltpu.make_async_remote_copy(
            hall.at[xs], hall.at[xs], gat_s, gat_r, device_id={"dp": x_of(q)}, device_id_type=MESH
        ).start()

    for ch in range(1, CH1):
        send_in(ch)

    def expand(small, rows, cols):
        left = (iota((rows, small.shape[0]), 0) // 16 == iota((rows, small.shape[0]), 1)).astype(F32).astype(BF)
        right = (iota((128, cols), 1) // 16 == iota((128, cols), 0)).astype(F32).astype(BF)
        tall = jnp.dot(left, small, preferred_element_type=F32).astype(BF)
        wide = jnp.dot(tall, right, preferred_element_type=F32)
        keep = lax.rem(iota((rows, cols), 0), 16) == lax.rem(iota((rows, cols), 1), 16)
        return jnp.where(keep, wide, 0.0).astype(BF)

    fone[...] = expand(first[...], 1024, 512)
    ftwo[...] = expand(last[...], 512, 1024)

    @pl.loop(0, 32)
    def _(k):
        ca, sa = cosa[pl.ds(k, 1), :], sina[pl.ds(k, 1), :]
        co = ca * cosb[...] - sa * sinb[...]
        si = sa * cosb[...] + ca * sinb[...]
        mats[k, 0:128, 0:128] = co.astype(BF)
        mats[k, 0:128, 128:256] = si.astype(BF)
        mats[k, 128:256, 0:128] = (-si).astype(BF)
        mats[k, 128:256, 128:256] = co.astype(BF)
        cot, sit = co.T, si.T
        matst[k, 0:128, 0:128] = cot.astype(BF)
        matst[k, 0:128, 128:256] = (-sit).astype(BF)
        matst[k, 128:256, 0:128] = sit.astype(BF)
        matst[k, 128:256, 128:256] = cot.astype(BF)

    def stage_one(x, g):
        y = jnp.dot(fone[...], x.reshape(512, 128), preferred_element_type=F32)
        ybuf[:, :, g] = y.astype(BF).reshape(32, 2, 16, 128)

    def stage_two(k):
        return jnp.dot(mats[k], ybuf[k].reshape(256, 128), preferred_element_type=F32)

    pltpu.make_async_copy(hall.at[0:3], hall.at[0:3], gat_r).wait()

    @pl.loop(0, NCTX)
    def _(a):
        block = hall[:, a].reshape(64, 128).astype(F32)
        turned = jnp.concatenate([block, block], axis=0).T
        htime[:, a] = turned.astype(BF).reshape(8, 16, 128)

    @pl.loop(0, GR)
    def _(g):
        stage_one(htime[g], g)

    wide_low = iota((128, 128), 1) < 64

    @pl.loop(0, 32)
    def _(k):
        s = stage_two(k)
        hspec[k, 0:128] = s[0:128]
        hspec[k, 128:256] = jnp.where(wide_low, s[128:256], -s[128:256])

    own_one.wait()
    for ch in range(CH1):
        part = recv1.at[per1 * ch:per1 * ch + per1, 0:31]
        pltpu.make_async_copy(part, part, one_r.at[ch]).wait()

        @pl.loop(per1 * ch, per1 * ch + per1)
        def _(g):
            stage_one(recv1[g], g)

    @pl.loop(0, 32)
    def _(k):
        s = stage_two(k)
        xspec[k] = s
        sr, si = s[0:128], s[128:256]
        hr, hi = hspec[k, 0:128], hspec[k, 128:256]
        p = jnp.concatenate([sr * hr - si * hi, sr * hi + si * hr], axis=0).astype(BF)
        v = jnp.dot(matst[k], p, preferred_element_type=F32).astype(BF).reshape(2, 8, 16, 128)
        vbuf[:, k, 0] = v[0]
        vbuf[:, k, 1] = v[1]

    gain = skip[pl.ds(me // 2, 1), :]
    turned_gain = pltpu.roll(jnp.broadcast_to(gain, (8, 128)), 64, axis=1)[0:1]
    low_row = iota((1, 128), 1) < 64
    even = jnp.where(low_row, gain, turned_gain)
    odd = jnp.where(low_row, turned_gain, gain)
    parity = lax.rem(me, 2).astype(F32)
    gain2 = even * (1.0 - parity) + odd * parity

    per2 = GR // CH2
    for ch in range(CH2):
        @pl.loop(per2 * ch, per2 * ch + per2)
        def _(g):
            o = jnp.dot(ftwo[...], vbuf[g].reshape(1024, 128), preferred_element_type=F32)
            o = o + gain2 * recv1[g].reshape(512, 128).astype(F32)
            send2[g] = o.astype(BF).reshape(32, 16, 128)

        span = slice(per2 * ch, per2 * ch + per2)

        @pl.loop(1, NCTX)
        def _(p):
            peer = peer_of(p)
            pltpu.make_async_remote_copy(
                send2.at[span, peer], recv2.at[span, me], two_s.at[ch], two_r.at[ch],
                device_id={"ctx": peer}, device_id_type=MESH,
            ).start()

    own_two = pltpu.make_async_copy(send2.at[:, me], recv2.at[:, me], own.at[2])
    own_two.start()

    @pl.loop(0, 32)
    def _(k):
        s = xspec[k]
        sr, si = s[0:128], s[128:256]
        gr, gi = swap(sr), swap(si)
        q = jnp.concatenate([sr * gr + si * gi, sr * gi - si * gr], axis=0).astype(BF)
        v = jnp.dot(matst[k], q, preferred_element_type=F32).reshape(2, 2, 64, 128)
        for c in range(2):
            both = jnp.where(iota((64, 128), 1) < 64, v[c, 0], swap(v[c, 1]))
            qbuf[:, k, c] = both.astype(BF).reshape(4, 16, 128)

    @pl.loop(0, 4)
    def _(g):
        o = jnp.dot(ftwo[...], qbuf[g].reshape(1024, 128), preferred_element_type=F32)
        dfs[:, g] = o.astype(BF).reshape(8, 4, 16, 128)

    @pl.loop(1, NDP)
    def _(q):
        other = dp_of(q)
        pltpu.make_async_remote_copy(
            dfs.at[other], dfr.at[dp], df_s, df_r, device_id={"dp": other}, device_id_type=MESH
        ).start()

    own_df = pltpu.make_async_copy(dfs.at[dp], dfr.at[dp], own.at[3])
    own_df.start()

    own_two.wait()
    for ch in range(CH2):
        part = recv2.at[per2 * ch:per2 * ch + per2, 0:31]
        pltpu.make_async_copy(part, part, two_r.at[ch]).wait()

        @pl.loop(per2 * ch, per2 * ch + per2)
        def _(g):
            rows = pl.ds(pl.multiple_of(16 * g, 16), 16)
            factor = scale[rows, :]
            for m in range(16):
                cols = slice(128 * m, 128 * m + 128)
                left, right = recv2[g, 2 * m].astype(F32), recv2[g, 2 * m + 1].astype(F32)
                z = jnp.where(low, left, swap(right))
                d_input[0, rows, cols] = jnp.where(low, swap(left), right).astype(BF)
                d_gate[0, rows, cols] = (grad[0, rows, cols].astype(F32) * factor * z).astype(BF)

    own_df.wait()
    pltpu.make_async_copy(dfr.at[0:7], dfr.at[0:7], df_r).wait()
    for a in range(4):
        total = dfr[0, :, a].astype(F32)
        for r in range(1, NDP):
            total = total + dfr[r, :, a].astype(F32)
        turned = total.reshape(64, 128).T
        d_filter[:, 128 * a:128 * a + 64] = turned[0:64]
        d_filter[:, 128 * a + 64:128 * a + 128] = turned[64:128]

    pltpu.make_async_copy(docs_all.at[0:31], docs_all.at[0:31], doc_s).wait()
    pltpu.make_async_copy(hall.at[0, 0:31], hall.at[0, 0:31], tap_s).wait()
    pltpu.make_async_copy(hall.at[0:3], hall.at[0:3], gat_s).wait()
    for ch in range(CH1):
        part = send1.at[per1 * ch:per1 * ch + per1, 0:31]
        pltpu.make_async_copy(part, part, one_s.at[ch]).wait()
    for ch in range(CH2):
        part = send2.at[per2 * ch:per2 * ch + per2, 0:31]
        pltpu.make_async_copy(part, part, two_s.at[ch]).wait()
    pltpu.make_async_copy(dfs.at[0:7], dfs.at[0:7], df_s).wait()


def local(grad_out, saved_input, gate_value, filter_taps, skip_gain, lang_ids, doc_ids, dro_weight):
    vmem = pl.BlockSpec(memory_space=pltpu.VMEM)
    dma = pltpu.SemaphoreType.DMA
    token = jax.ShapeDtypeStruct((1, 128, 2048), BF)
    return pl.pallas_call(
        kernel,
        out_shape=(token, token, jax.ShapeDtypeStruct((64, 512), F32)),
        in_specs=[vmem] * 7 + [pl.BlockSpec(memory_space=pltpu.SMEM)] + [vmem] * 6,
        out_specs=(vmem, vmem, vmem),
        scratch_shapes=[
            pltpu.VMEM((8, 128), jnp.int32),
            pltpu.VMEM((NCTX, 8, 128), jnp.int32),
            pltpu.VMEM((NX, NCTX, 16, 128), BF),
            pltpu.VMEM((GR, NCTX, 16, 128), BF),
            pltpu.VMEM((128, 128), F32),
            pltpu.VMEM((32, 256, 256), BF),
            pltpu.VMEM((32, 256, 256), BF),
            pltpu.VMEM((1024, 512), BF),
            pltpu.VMEM((512, 1024), BF),
            pltpu.VMEM((GR, NCTX, 16, 128), BF),
            pltpu.VMEM((GR, NCTX, 16, 128), BF),
            pltpu.VMEM((GR, NCTX, 16, 128), BF),
            pltpu.VMEM((GR, NCTX, 16, 128), BF),
            pltpu.VMEM((32, 2, GR, 16, 128), BF),
            pltpu.VMEM((GR, 32, 2, 16, 128), BF),
            pltpu.VMEM((4, 32, 2, 16, 128), BF),
            pltpu.VMEM((32, 256, 128), F32),
            pltpu.VMEM((32, 256, 128), F32),
            pltpu.VMEM((NDP, 4, 4, 16, 128), BF),
            pltpu.VMEM((NDP, 4, 4, 16, 128), BF),
            dma, dma, dma, dma, dma, dma,
            dma((CH1,)), dma((CH1,)), dma((CH2,)), dma((CH2,)),
            dma, dma, dma((4,)),
        ],
        compiler_params=pltpu.CompilerParams(
            collective_id=0, has_side_effects=True, vmem_limit_bytes=56 << 20
        ),
        name="hyena_backward",
    )(
        grad_out, saved_input, gate_value, filter_taps, skip_gain.reshape(16, 128), lang_ids, doc_ids, dro_weight,
        *tables(),
    )


def solution(mesh):
    return jax.shard_map(
        local,
        mesh=mesh,
        in_specs=(
            P("dp", "ctx", None), P("dp", "ctx", None), P("dp", "ctx", None), P(None, "ctx"),
            P(), P("dp", "ctx"), P("dp", "ctx"), P(),
        ),
        out_specs=(P("dp", "ctx", None), P("dp", "ctx", None), P("ctx", "dp")),
        check_vma=False,
    )
```

```python
import functools
import math

import jax
import jax.numpy as jnp
import numpy as np
from jax import lax
from jax.experimental import pallas as pl
from jax.experimental.pallas import tpu as pltpu
from jax.sharding import PartitionSpec as P

MESH = pl.DeviceIdType.MESH
BF = jnp.bfloat16
F32 = jnp.float32
NCTX, NDP, NX = 32, 8, 4
LEN = 4096
GR = 8
CU, CD, CO = 2, 4, 8
UN = 8
UQ = 4
SPLIT = 4


def tables():
    k1 = np.arange(32)
    a = np.arange(32)
    b = np.arange(128)
    phi = 2 * math.pi / 128 * ((a[None, :] * (4 * k1[:, None] + 1)) % 128)
    first = np.zeros((64, 128), np.float32)
    first[:, :32] = np.stack([np.cos(phi), -np.sin(phi)], 1).reshape(64, 32)
    last = np.zeros((32, 128), np.float32)
    last[:, :64] = first[:, :32].T / LEN
    alpha = 2 * math.pi / 16384 * ((b[None, :] * (4 * k1[:, None] + 1)) % 16384)
    beta = 2 * math.pi / 128 * ((b[None, :] * b[:, None]) % 128)
    f = lambda v: jnp.asarray(v.astype(np.float32))
    return (
        jnp.asarray(first, BF),
        jnp.asarray(last, BF),
        f(np.cos(alpha)),
        f(np.sin(alpha)),
        f(np.cos(beta)),
        f(np.sin(beta)),
    )


def iota(shape, dim):
    return lax.broadcasted_iota(jnp.int32, shape, dim)


def swap(x):
    return pltpu.roll(x, 64, axis=1)


def kernel(
    grad, sig, gate, taps, skip, lang, docs, dro, first, last, cosa, sina, cosb, sinb,
    d_input, d_gate, d_filter,
    docs_out, docs_all, hall, htime, scale, mats, matst, fone, ftwo, sendu, recvu, sendd, recvd, xin, send2, recv2,
    ybuf, vbuf, qbuf, hspec, xspec, dfs, dfr,
    doc_s, doc_r, tap_s, tap_r, gat_s, gat_r, u_s, u_r, d_s, d_r, two_s, two_r, df_s, df_r, own,
):
    me = lax.axis_index("ctx")
    dp = lax.axis_index("dp")
    xs = lax.rem(dp, NX)
    zl = dp // NX
    low = iota((16, 128), 1) < 64

    def peer_of(p):
        return lax.rem(me + p, NCTX)

    def dp_of(q):
        return lax.rem(dp + q, NDP)

    def x_of(q):
        return zl * NX + lax.rem(xs + q, NX)

    barrier = pltpu.get_barrier_semaphore()

    @pl.loop(1, NCTX)
    def _(p):
        pl.semaphore_signal(barrier, inc=1, device_id={"ctx": peer_of(p)}, device_id_type=MESH)

    @pl.loop(1, NDP)
    def _(q):
        pl.semaphore_signal(barrier, inc=1, device_id={"dp": dp_of(q)}, device_id_type=MESH)

    def pair_store(dst, g, m, first_half, second_half):
        dst[g, 2 * m] = jnp.where(low, first_half, swap(second_half)).astype(BF)
        dst[g, 2 * m + 1] = jnp.where(low, swap(first_half), second_half).astype(BF)

    def rows_of(g):
        return pl.ds(pl.multiple_of(16 * g, 16), 16)

    docs_row = docs[...]
    docs_out[...] = jnp.broadcast_to(docs_row, (8, 128))
    docs_all[me] = jnp.broadcast_to(docs_row, (8, 128))

    @pl.loop(0, 4)
    def _(g):
        for m in range(16):
            cols = slice(128 * m, 128 * m + 128)
            pair_store(sendu, g, m, sig[0, rows_of(g), cols].astype(F32), sig[0, rows_of(g + 4), cols].astype(F32))

    pl.semaphore_wait(barrier, NCTX - 1 + NDP - 1)

    @pl.loop(1, NCTX)
    def _(p):
        peer = peer_of(p)
        pltpu.make_async_remote_copy(
            docs_out, docs_all.at[me], doc_s, doc_r, device_id={"ctx": peer}, device_id_type=MESH
        ).start()

    def tap_rows(j):
        return taps.at[pl.ds(pl.multiple_of(64 * j + 16 * xs, 16), 16), :]

    @pl.loop(1, NCTX)
    def _(p):
        peer = peer_of(p)
        pltpu.make_async_remote_copy(
            tap_rows(peer), hall.at[xs, me], tap_s, tap_r, device_id={"ctx": peer}, device_id_type=MESH
        ).start()

    own_taps = pltpu.make_async_copy(tap_rows(me), hall.at[xs, me], own.at[0])
    own_taps.start()

    def spread(src, dst, chunk, chunks, sems, semr):
        per = src.shape[0] // chunks
        span = slice(per * chunk, per * chunk + per)

        @pl.loop(1, NCTX)
        def _(p):
            peer = peer_of(p)
            pltpu.make_async_remote_copy(
                src.at[span, peer], dst.at[span, me], sems.at[chunk], semr.at[chunk],
                device_id={"ctx": peer}, device_id_type=MESH,
            ).start()

    def await_all(buf, chunk, chunks, sem):
        per = buf.shape[0] // chunks
        part = buf.at[per * chunk:per * chunk + per, 0:31]
        pltpu.make_async_copy(part, part, sem.at[chunk]).wait()

    spread(sendu, recvu, 0, CU, u_s, u_r)

    def column(row):
        return jnp.broadcast_to(row.astype(F32), (128, 128)).T

    own_docs = column(docs_row)
    own_lang = column(lang[...])
    weight = jnp.zeros((128, 128), F32)
    for group in range(16):
        weight = jnp.where(own_lang == float(group), dro[group], weight)
    pltpu.make_async_copy(docs_all.at[0:31], docs_all.at[0:31], doc_r).wait()

    def count(a, total):
        row = jnp.broadcast_to(docs_all[a][0:1].astype(F32), (128, 128))
        return total + jnp.where(row == own_docs, 1.0, 0.0)

    hits = lax.fori_loop(0, NCTX, count, jnp.zeros((128, 128), F32))
    doc_len = jnp.sum(hits, axis=1, keepdims=True)
    scale[...] = weight * 256.0 / (doc_len + 128.0)

    own_taps.wait()
    pltpu.make_async_copy(hall.at[0, 0:31], hall.at[0, 0:31], tap_r).wait()

    @pl.loop(1, NX)
    def _(q):
        pltpu.make_async_remote_copy(
            hall.at[xs], hall.at[xs], gat_s, gat_r, device_id={"dp": x_of(q)}, device_id_type=MESH
        ).start()

    for ch in range(1, CU):
        spread(sendu, recvu, ch, CU, u_s, u_r)

    for ch in range(CD):
        @pl.loop(4 // CD * ch, 4 // CD * ch + 4 // CD)
        def _(g):
            for m in range(16):
                cols = slice(128 * m, 128 * m + 128)
                halves = []
                for h in range(2):
                    rows = rows_of(g + 4 * h)
                    dy = grad[0, rows, cols].astype(F32) * scale[rows, :]
                    halves.append(dy * gate[0, rows, cols].astype(F32))
                pair_store(sendd, g, m, *halves)

        spread(sendd, recvd, ch, CD, d_s, d_r)

    own_u = pltpu.make_async_copy(sendu.at[:, me], recvu.at[:, me], own.at[1])
    own_u.start()
    own_d = pltpu.make_async_copy(sendd.at[:, me], recvd.at[:, me], own.at[4])
    own_d.start()

    def expand(small, rows, cols):
        left = (iota((rows, small.shape[0]), 0) // 16 == iota((rows, small.shape[0]), 1)).astype(F32).astype(BF)
        right = (iota((128, cols), 1) // 16 == iota((128, cols), 0)).astype(F32).astype(BF)
        tall = jnp.dot(left, small, preferred_element_type=F32).astype(BF)
        wide = jnp.dot(tall, right, preferred_element_type=F32)
        keep = lax.rem(iota((rows, cols), 0), 16) == lax.rem(iota((rows, cols), 1), 16)
        return jnp.where(keep, wide, 0.0).astype(BF)

    fone[...] = expand(first[...], 1024, 512)
    ftwo[...] = expand(last[...], 512, 1024)

    @pl.loop(0, 32)
    def _(k):
        ca, sa = cosa[pl.ds(k, 1), :], sina[pl.ds(k, 1), :]
        co = ca * cosb[...] - sa * sinb[...]
        si = sa * cosb[...] + ca * sinb[...]
        mats[k, 0:128, 0:128] = co.astype(BF)
        mats[k, 0:128, 128:256] = si.astype(BF)
        mats[k, 128:256, 0:128] = (-si).astype(BF)
        mats[k, 128:256, 128:256] = co.astype(BF)
        cot, sit = co.T, si.T
        matst[k, 0:128, 0:128] = cot.astype(BF)
        matst[k, 0:128, 128:256] = (-sit).astype(BF)
        matst[k, 128:256, 0:128] = sit.astype(BF)
        matst[k, 128:256, 128:256] = cot.astype(BF)

    def stage_one(x, g):
        y = jnp.dot(fone[...], x.reshape(512, 128), preferred_element_type=F32)
        ybuf[:, :, g] = y.astype(BF).reshape(32, 2, 16, 128)

    def stage_two(k):
        return jnp.dot(mats[k], ybuf[k].reshape(256, 128), preferred_element_type=F32)

    pltpu.make_async_copy(hall.at[0:3], hall.at[0:3], gat_r).wait()

    @pl.loop(0, NCTX)
    def _(a):
        block = hall[:, a].reshape(64, 128).astype(F32)
        turned = jnp.concatenate([block, block], axis=0).T
        htime[:, a] = turned.astype(BF).reshape(8, 16, 128)

    @pl.loop(0, GR)
    def _(g):
        stage_one(htime[g], g)

    wide_low = iota((128, 128), 1) < 64

    @pl.loop(0, 32, unroll=UQ)
    def _(k):
        s = stage_two(k)
        hspec[k, 0:128] = s[0:128]
        hspec[k, 128:256] = jnp.where(wide_low, s[128:256], -s[128:256])

    own_u.wait()
    own_d.wait()
    for ch in range(CU):
        await_all(recvu, ch, CU, u_r)
    tall_low = iota((512, 128), 1) < 64
    for ch in range(CD):
        await_all(recvd, ch, CD, d_r)

        @pl.loop(4 // CD * ch, 4 // CD * ch + 4 // CD)
        def _(g):
            u = recvu[g].reshape(512, 128).astype(F32)
            d = recvd[g].reshape(512, 128).astype(F32)
            first_half = jnp.where(tall_low, u, swap(d)).astype(BF).reshape(32, 16, 128)
            second_half = jnp.where(tall_low, swap(u), d).astype(BF).reshape(32, 16, 128)
            xin[g] = first_half
            xin[g + 4] = second_half
            stage_one(first_half, g)
            stage_one(second_half, g + 4)

    @pl.loop(0, 32, unroll=UN)
    def _(k):
        s = stage_two(k)
        xspec[k] = s
        sr, si = s[0:128], s[128:256]
        hr, hi = hspec[k, 0:128], hspec[k, 128:256]
        p = jnp.concatenate([sr * hr - si * hi, sr * hi + si * hr], axis=0).astype(BF)
        v = jnp.dot(matst[k], p, preferred_element_type=F32).astype(BF).reshape(2, 8, 16, 128)
        vbuf[:, k, 0] = v[0]
        vbuf[:, k, 1] = v[1]

    gain = skip[pl.ds(me // 2, 1), :]
    turned_gain = pltpu.roll(jnp.broadcast_to(gain, (8, 128)), 64, axis=1)[0:1]
    low_row = iota((1, 128), 1) < 64
    even = jnp.where(low_row, gain, turned_gain)
    odd = jnp.where(low_row, turned_gain, gain)
    parity = lax.rem(me, 2).astype(F32)
    gain2 = even * (1.0 - parity) + odd * parity

    per2 = GR // CO

    def send_back(ch):
        @pl.loop(per2 * ch, per2 * ch + per2)
        def _(g):
            o = jnp.dot(ftwo[...], vbuf[g].reshape(1024, 128), preferred_element_type=F32)
            o = o + gain2 * xin[g].reshape(512, 128).astype(F32)
            send2[g] = o.astype(BF).reshape(32, 16, 128)

        spread(send2, recv2, ch, CO, two_s, two_r)

    for ch in range(SPLIT):
        send_back(ch)

    @pl.loop(0, 32, unroll=UQ)
    def _(k):
        s = xspec[k]
        sr, si = s[0:128], s[128:256]
        gr, gi = swap(sr), swap(si)
        q = jnp.concatenate([sr * gr + si * gi, sr * gi - si * gr], axis=0).astype(BF)
        v = jnp.dot(matst[k], q, preferred_element_type=F32).reshape(2, 2, 64, 128)
        for c in range(2):
            both = jnp.where(iota((64, 128), 1) < 64, v[c, 0], swap(v[c, 1]))
            qbuf[:, k, c] = both.astype(BF).reshape(4, 16, 128)

    @pl.loop(0, 4)
    def _(g):
        o = jnp.dot(ftwo[...], qbuf[g].reshape(1024, 128), preferred_element_type=F32)
        dfs[:, g] = o.astype(BF).reshape(8, 4, 16, 128)

    @pl.loop(1, NDP)
    def _(q):
        other = dp_of(q)
        pltpu.make_async_remote_copy(
            dfs.at[other], dfr.at[dp], df_s, df_r, device_id={"dp": other}, device_id_type=MESH
        ).start()

    own_df = pltpu.make_async_copy(dfs.at[dp], dfr.at[dp], own.at[3])
    own_df.start()

    for ch in range(SPLIT, CO):
        send_back(ch)

    own_two = pltpu.make_async_copy(send2.at[:, me], recv2.at[:, me], own.at[2])
    own_two.start()

    own_two.wait()
    for ch in range(CO):
        await_all(recv2, ch, CO, two_r)

        @pl.loop(per2 * ch, per2 * ch + per2)
        def _(g):
            rows = pl.ds(pl.multiple_of(16 * g, 16), 16)
            factor = scale[rows, :]
            for m in range(16):
                cols = slice(128 * m, 128 * m + 128)
                left, right = recv2[g, 2 * m].astype(F32), recv2[g, 2 * m + 1].astype(F32)
                z = jnp.where(low, left, swap(right))
                d_input[0, rows, cols] = jnp.where(low, swap(left), right).astype(BF)
                d_gate[0, rows, cols] = (grad[0, rows, cols].astype(F32) * factor * z).astype(BF)

    own_df.wait()
    pltpu.make_async_copy(dfr.at[0:7], dfr.at[0:7], df_r).wait()
    for a in range(4):
        total = dfr[0, :, a].astype(F32)
        for r in range(1, NDP):
            total = total + dfr[r, :, a].astype(F32)
        turned = total.reshape(64, 128).T
        d_filter[:, 128 * a:128 * a + 64] = turned[0:64]
        d_filter[:, 128 * a + 64:128 * a + 128] = turned[64:128]

    pltpu.make_async_copy(docs_all.at[0:31], docs_all.at[0:31], doc_s).wait()
    pltpu.make_async_copy(hall.at[0, 0:31], hall.at[0, 0:31], tap_s).wait()
    pltpu.make_async_copy(hall.at[0:3], hall.at[0:3], gat_s).wait()
    for ch in range(CU):
        await_all(sendu, ch, CU, u_s)
    for ch in range(CD):
        await_all(sendd, ch, CD, d_s)
    for ch in range(CO):
        await_all(send2, ch, CO, two_s)
    pltpu.make_async_copy(dfs.at[0:7], dfs.at[0:7], df_s).wait()


def local(grad_out, saved_input, gate_value, filter_taps, skip_gain, lang_ids, doc_ids, dro_weight):
    vmem = pl.BlockSpec(memory_space=pltpu.VMEM)
    dma = pltpu.SemaphoreType.DMA
    token = jax.ShapeDtypeStruct((1, 128, 2048), BF)
    return pl.pallas_call(
        kernel,
        out_shape=(token, token, jax.ShapeDtypeStruct((64, 512), F32)),
        in_specs=[vmem] * 7 + [pl.BlockSpec(memory_space=pltpu.SMEM)] + [vmem] * 6,
        out_specs=(vmem, vmem, vmem),
        scratch_shapes=[
            pltpu.VMEM((8, 128), jnp.int32),
            pltpu.VMEM((NCTX, 8, 128), jnp.int32),
            pltpu.VMEM((NX, NCTX, 16, 128), BF),
            pltpu.VMEM((GR, NCTX, 16, 128), BF),
            pltpu.VMEM((128, 128), F32),
            pltpu.VMEM((32, 256, 256), BF),
            pltpu.VMEM((32, 256, 256), BF),
            pltpu.VMEM((1024, 512), BF),
            pltpu.VMEM((512, 1024), BF),
            pltpu.VMEM((4, NCTX, 16, 128), BF),
            pltpu.VMEM((4, NCTX, 16, 128), BF),
            pltpu.VMEM((4, NCTX, 16, 128), BF),
            pltpu.VMEM((4, NCTX, 16, 128), BF),
            pltpu.VMEM((GR, NCTX, 16, 128), BF),
            pltpu.VMEM((GR, NCTX, 16, 128), BF),
            pltpu.VMEM((GR, NCTX, 16, 128), BF),
            pltpu.VMEM((32, 2, GR, 16, 128), BF),
            pltpu.VMEM((GR, 32, 2, 16, 128), BF),
            pltpu.VMEM((4, 32, 2, 16, 128), BF),
            pltpu.VMEM((32, 256, 128), F32),
            pltpu.VMEM((32, 256, 128), F32),
            pltpu.VMEM((NDP, 4, 4, 16, 128), BF),
            pltpu.VMEM((NDP, 4, 4, 16, 128), BF),
            dma, dma, dma, dma, dma, dma,
            dma((CU,)), dma((CU,)), dma((CD,)), dma((CD,)), dma((CO,)), dma((CO,)),
            dma, dma, dma((5,)),
        ],
        compiler_params=pltpu.CompilerParams(
            collective_id=0, has_side_effects=True, vmem_limit_bytes=56 << 20
        ),
        name="hyena_backward",
    )(
        grad_out, saved_input, gate_value, filter_taps, skip_gain.reshape(16, 128), lang_ids, doc_ids, dro_weight,
        *tables(),
    )


def solution(mesh):
    return jax.shard_map(
        local,
        mesh=mesh,
        in_specs=(
            P("dp", "ctx", None), P("dp", "ctx", None), P("dp", "ctx", None), P(None, "ctx"),
            P(), P("dp", "ctx"), P("dp", "ctx"), P(),
        ),
        out_specs=(P("dp", "ctx", None), P("dp", "ctx", None), P("ctx", "dp")),
        check_vma=False,
    )
```

```python
import functools
import math

import jax
import jax.numpy as jnp
import numpy as np
from jax import lax
from jax.experimental import pallas as pl
from jax.experimental.pallas import tpu as pltpu
from jax.sharding import PartitionSpec as P

MESH = pl.DeviceIdType.MESH
BF = jnp.bfloat16
F32 = jnp.float32
NCTX, NDP, NX = 32, 8, 4
LEN = 4096
CC = (2, 2)
FIRST = 1
GR = 8
CI, CO = CC
UN = 8
UQ = 4


def tables():
    k1 = np.arange(32)
    a = np.arange(32)
    b = np.arange(128)
    phi = 2 * math.pi / 128 * ((a[None, :] * (4 * k1[:, None] + 1)) % 128)
    first = np.zeros((64, 128), np.float32)
    first[:, :32] = np.stack([np.cos(phi), -np.sin(phi)], 1).reshape(64, 32)
    last = np.zeros((32, 128), np.float32)
    last[:, :64] = first[:, :32].T / LEN
    alpha = 2 * math.pi / 16384 * ((b[None, :] * (4 * k1[:, None] + 1)) % 16384)
    beta = 2 * math.pi / 128 * ((b[None, :] * b[:, None]) % 128)
    f = lambda v: jnp.asarray(v.astype(np.float32))
    return (
        jnp.asarray(first, BF),
        jnp.asarray(last, BF),
        f(np.cos(alpha)),
        f(np.sin(alpha)),
        f(np.cos(beta)),
        f(np.sin(beta)),
    )


def iota(shape, dim):
    return lax.broadcasted_iota(jnp.int32, shape, dim)


def swap(x):
    return pltpu.roll(x, 64, axis=1)


def kernel(
    grad, sig, gate, taps, skip, lang, docs, dro, first, last, cosa, sina, cosb, sinb,
    d_input, d_gate, d_filter,
    docs_out, docs_all, hall, htime, scale, mats, matst, fone, ftwo, sendu, recvu, sendd, recvd, sendz, recvz,
    sendi, recvi, ybuf, vbuf, qbuf, hspec, uspec, gspec, dfs, dfr, dft, dfq,
    doc_s, doc_r, tap_s, tap_r, gat_s, gat_r, u_s, u_r, d_s, d_r, z_s, z_r, i_s, i_r, df_s, df_r, dq_s, dq_r, own,
):
    me = lax.axis_index("ctx")
    dp = lax.axis_index("dp")
    xs = lax.rem(dp, NX)
    zl = dp // NX
    low = iota((16, 128), 1) < 64

    def peer_of(p):
        return lax.rem(me + p, NCTX)

    def x_of(q):
        return zl * NX + lax.rem(xs + q, NX)

    barrier = pltpu.get_barrier_semaphore()

    @pl.loop(1, NCTX)
    def _(p):
        pl.semaphore_signal(barrier, inc=1, device_id={"ctx": peer_of(p)}, device_id_type=MESH)

    across = lax.rem(dp + NX, NDP)

    @pl.loop(1, NX)
    def _(q):
        pl.semaphore_signal(barrier, inc=1, device_id={"dp": x_of(q)}, device_id_type=MESH)

    pl.semaphore_signal(barrier, inc=1, device_id={"dp": across}, device_id_type=MESH)

    def pair_store(dst, g, m, first_half, second_half):
        dst[g, 2 * m] = jnp.where(low, first_half, swap(second_half)).astype(BF)
        dst[g, 2 * m + 1] = jnp.where(low, swap(first_half), second_half).astype(BF)

    def rows_of(g):
        return pl.ds(pl.multiple_of(16 * g, 16), 16)

    docs_row = docs[...]
    docs_out[...] = docs_row
    docs_all[me] = docs_row

    @pl.loop(0, 4)
    def _(g):
        for m in range(16):
            cols = slice(128 * m, 128 * m + 128)
            pair_store(sendu, g, m, sig[0, rows_of(g), cols].astype(F32), sig[0, rows_of(g + 4), cols].astype(F32))

    pl.semaphore_wait(barrier, NCTX - 1 + NX)

    @pl.loop(1, NCTX)
    def _(p):
        peer = peer_of(p)
        pltpu.make_async_remote_copy(
            docs_out, docs_all.at[me], doc_s, doc_r, device_id={"ctx": peer}, device_id_type=MESH
        ).start()

    def tap_rows(j):
        return taps.at[pl.ds(pl.multiple_of(64 * j + 16 * xs, 16), 16), :]

    @pl.loop(1, NCTX)
    def _(p):
        peer = peer_of(p)
        pltpu.make_async_remote_copy(
            tap_rows(peer), hall.at[xs, me], tap_s, tap_r, device_id={"ctx": peer}, device_id_type=MESH
        ).start()

    own_taps = pltpu.make_async_copy(tap_rows(me), hall.at[xs, me], own.at[0])
    own_taps.start()

    def spread(src, dst, chunk, chunks, sems, semr):
        per = src.shape[0] // chunks
        span = slice(per * chunk, per * chunk + per)

        @pl.loop(1, NCTX)
        def _(p):
            peer = peer_of(p)
            pltpu.make_async_remote_copy(
                src.at[span, peer], dst.at[span, me], sems.at[chunk], semr.at[chunk],
                device_id={"ctx": peer}, device_id_type=MESH,
            ).start()

    def await_all(buf, chunk, chunks, sem):
        per = buf.shape[0] // chunks
        part = buf.at[per * chunk:per * chunk + per, 0:31]
        pltpu.make_async_copy(part, part, sem.at[chunk]).wait()

    spread(sendu, recvu, 0, CI, u_s, u_r)

    own_taps.wait()
    pltpu.make_async_copy(hall.at[0, 0:31], hall.at[0, 0:31], tap_r).wait()

    @pl.loop(1, NX)
    def _(q):
        pltpu.make_async_remote_copy(
            hall.at[xs], hall.at[xs], gat_s, gat_r, device_id={"dp": x_of(q)}, device_id_type=MESH
        ).start()

    for ch in range(1, CI):
        spread(sendu, recvu, ch, CI, u_s, u_r)

    def column(row):
        return jnp.broadcast_to(row.astype(F32), (128, 128)).T

    own_docs = column(docs_row)
    own_lang = column(lang[...])
    weight = jnp.zeros((128, 128), F32)
    for group in range(16):
        weight = jnp.where(own_lang == float(group), dro[group], weight)
    pltpu.make_async_copy(docs_all.at[0:31], docs_all.at[0:31], doc_r).wait()

    def count(a, total):
        row = jnp.broadcast_to(docs_all[a].astype(F32), (128, 128))
        return total + jnp.where(row == own_docs, 1.0, 0.0)

    hits = lax.fori_loop(0, NCTX, count, jnp.zeros((128, 128), F32))
    doc_len = jnp.sum(hits, axis=1, keepdims=True)
    scale[...] = weight * 256.0 / (doc_len + 128.0)

    for ch in range(CI):
        @pl.loop(4 // CI * ch, 4 // CI * ch + 4 // CI)
        def _(g):
            for m in range(16):
                cols = slice(128 * m, 128 * m + 128)
                halves = []
                for h in range(2):
                    rows = rows_of(g + 4 * h)
                    dy = grad[0, rows, cols].astype(F32) * scale[rows, :]
                    halves.append(dy * gate[0, rows, cols].astype(F32))
                pair_store(sendd, g, m, *halves)

        spread(sendd, recvd, ch, CI, d_s, d_r)

    own_u = pltpu.make_async_copy(sendu.at[:, me], recvu.at[:, me], own.at[1])
    own_u.start()
    own_d = pltpu.make_async_copy(sendd.at[:, me], recvd.at[:, me], own.at[4])
    own_d.start()

    def expand(small, rows, cols):
        left = (iota((rows, small.shape[0]), 0) // 16 == iota((rows, small.shape[0]), 1)).astype(F32).astype(BF)
        right = (iota((128, cols), 1) // 16 == iota((128, cols), 0)).astype(F32).astype(BF)
        tall = jnp.dot(left, small, preferred_element_type=F32).astype(BF)
        wide = jnp.dot(tall, right, preferred_element_type=F32)
        keep = lax.rem(iota((rows, cols), 0), 16) == lax.rem(iota((rows, cols), 1), 16)
        return jnp.where(keep, wide, 0.0).astype(BF)

    fone[...] = expand(first[...], 1024, 512)
    ftwo[...] = expand(last[...], 512, 1024)

    @pl.loop(0, 32)
    def _(k):
        ca, sa = cosa[pl.ds(k, 1), :], sina[pl.ds(k, 1), :]
        co = ca * cosb[...] - sa * sinb[...]
        si = sa * cosb[...] + ca * sinb[...]
        mats[k, 0:128, 0:128] = co.astype(BF)
        mats[k, 0:128, 128:256] = si.astype(BF)
        mats[k, 128:256, 0:128] = (-si).astype(BF)
        mats[k, 128:256, 128:256] = co.astype(BF)
        cot, sit = co.T, si.T
        matst[k, 0:128, 0:128] = cot.astype(BF)
        matst[k, 0:128, 128:256] = (-sit).astype(BF)
        matst[k, 128:256, 0:128] = sit.astype(BF)
        matst[k, 128:256, 128:256] = cot.astype(BF)

    def stage_one(x, g):
        y = jnp.dot(fone[...], x.reshape(512, 128), preferred_element_type=F32)
        ybuf[:, :, g] = y.astype(BF).reshape(32, 2, 16, 128)
        ybuf[:, :, g + 4] = swap(y).astype(BF).reshape(32, 2, 16, 128)

    def stage_two(k):
        return jnp.dot(mats[k], ybuf[k].reshape(256, 128), preferred_element_type=F32)

    pltpu.make_async_copy(hall.at[0:3], hall.at[0:3], gat_r).wait()

    @pl.loop(0, NCTX, unroll=2)
    def _(a):
        block = hall[:, a].reshape(64, 128).astype(F32)
        turned = jnp.concatenate([block, swap(block)], axis=0).T
        htime[:, a] = turned[0:64].astype(BF).reshape(4, 16, 128)

    @pl.loop(0, 4)
    def _(g):
        stage_one(htime[g], g)

    @pl.loop(0, 32, unroll=UQ)
    def _(k):
        hspec[k] = stage_two(k)

    gain = skip[pl.ds(me // 2, 1), :]
    turned_gain = pltpu.roll(jnp.broadcast_to(gain, (8, 128)), 64, axis=1)[0:1]
    low_row = iota((1, 128), 1) < 64
    even = jnp.where(low_row, gain, turned_gain)
    odd = jnp.where(low_row, turned_gain, gain)
    parity = lax.rem(me, 2).astype(F32)
    gain2 = even * (1.0 - parity) + odd * parity
    half_low = iota((64, 128), 1) < 64

    def invert(k, p, buf):
        v = jnp.dot(matst[k], p.astype(BF), preferred_element_type=F32).reshape(2, 2, 64, 128)
        for c in range(2):
            both = jnp.where(half_low, v[c, 0], swap(v[c, 1]))
            buf[:, k, c] = both.astype(BF).reshape(4, 16, 128)

    def bring(recv, local_copy, sem):
        local_copy.wait()
        for ch in range(CI):
            await_all(recv, ch, CI, sem)

            @pl.loop(4 // CI * ch, 4 // CI * ch + 4 // CI)
            def _(g):
                stage_one(recv[g], g)

    def send_back(source, send, recv, chunks, sems, semr):
        for ch in chunks:
            @pl.loop(4 // CO * ch, 4 // CO * ch + 4 // CO)
            def _(g):
                o = jnp.dot(ftwo[...], vbuf[g].reshape(1024, 128), preferred_element_type=F32)
                o = o + gain2 * source[g].reshape(512, 128).astype(F32)
                send[g] = o.astype(BF).reshape(32, 16, 128)

            spread(send, recv, ch, CO, sems, semr)

    bring(recvu, own_u, u_r)

    @pl.loop(0, 32, unroll=UN)
    def _(k):
        s = stage_two(k)
        uspec[k] = s
        sr, si = s[0:128], s[128:256]
        hr, hi = hspec[k, 0:128], hspec[k, 128:256]
        invert(k, jnp.concatenate([sr * hr - si * hi, sr * hi + si * hr], axis=0), vbuf)

    send_back(recvu, sendz, recvz, range(CO), z_s, z_r)
    own_z = pltpu.make_async_copy(sendz.at[:, me], recvz.at[:, me], own.at[2])
    own_z.start()

    bring(recvd, own_d, d_r)

    @pl.loop(0, 32, unroll=UN)
    def _(k):
        s = stage_two(k)
        gspec[k] = s
        sr, si = s[0:128], s[128:256]
        hr, hi = hspec[k, 0:128], hspec[k, 128:256]
        invert(k, jnp.concatenate([sr * hr + si * hi, si * hr - sr * hi], axis=0), vbuf)

    send_back(recvd, sendi, recvi, range(FIRST), i_s, i_r)

    @pl.loop(0, 32, unroll=UN)
    def _(k):
        sr, si = gspec[k, 0:128], gspec[k, 128:256]
        ur, ui = uspec[k, 0:128], uspec[k, 128:256]
        invert(k, jnp.concatenate([sr * ur + si * ui, si * ur - sr * ui], axis=0), qbuf)

    @pl.loop(0, 4)
    def _(g):
        o = jnp.dot(ftwo[...], qbuf[g].reshape(1024, 128), preferred_element_type=F32)
        o = o.astype(BF).reshape(2, 4, 4, 16, 128)
        dfs[:, 0, g] = o[0]
        dfs[:, 1, g] = o[1]

    @pl.loop(1, NX)
    def _(q):
        other = lax.rem(xs + q, NX)
        pltpu.make_async_remote_copy(
            dfs.at[other], dfr.at[xs], df_s, df_r, device_id={"dp": x_of(q)}, device_id_type=MESH
        ).start()

    own_df = pltpu.make_async_copy(dfs.at[xs], dfr.at[xs], own.at[3])
    own_df.start()
    send_back(recvd, sendi, recvi, range(FIRST, CO), i_s, i_r)
    own_i = pltpu.make_async_copy(sendi.at[:, me], recvi.at[:, me], own.at[0])
    own_i.start()

    own_df.wait()
    pltpu.make_async_copy(dfr.at[0:3], dfr.at[0:3], df_r).wait()

    def x_sum(zside):
        total = dfr[0, zside].astype(F32)
        for r in range(1, NX):
            total = total + dfr[r, zside].astype(F32)
        return total

    dft[...] = x_sum(1 - zl).astype(BF)
    swap_df = pltpu.make_async_remote_copy(
        dft, dfq, dq_s, dq_r, device_id={"dp": across}, device_id_type=MESH
    )
    swap_df.start()
    own_z.wait()
    own_i.wait()

    def unpair(recv, g, m):
        left, right = recv[g, 2 * m].astype(F32), recv[g, 2 * m + 1].astype(F32)
        return jnp.where(low, left, swap(right)), jnp.where(low, swap(left), right)

    for ch in range(CO):
        await_all(recvz, ch, CO, z_r)

        @pl.loop(4 // CO * ch, 4 // CO * ch + 4 // CO)
        def _(g):
            for m in range(16):
                cols = slice(128 * m, 128 * m + 128)
                for h, z in enumerate(unpair(recvz, g, m)):
                    rows = rows_of(g + 4 * h)
                    d_gate[0, rows, cols] = (grad[0, rows, cols].astype(F32) * scale[rows, :] * z).astype(BF)

    for ch in range(CO):
        await_all(recvi, ch, CO, i_r)

        @pl.loop(4 // CO * ch, 4 // CO * ch + 4 // CO)
        def _(g):
            for m in range(16):
                cols = slice(128 * m, 128 * m + 128)
                for h, v in enumerate(unpair(recvi, g, m)):
                    d_input[0, rows_of(g + 4 * h), cols] = v.astype(BF)

    swap_df.wait_recv()
    final = x_sum(zl) + dfq[...].astype(F32)
    for a in range(4):
        turned = final[:, a].reshape(64, 128).T
        d_filter[:, 128 * a:128 * a + 64] = turned[0:64]
        d_filter[:, 128 * a + 64:128 * a + 128] = turned[64:128]

    pltpu.make_async_copy(docs_all.at[0:31], docs_all.at[0:31], doc_s).wait()
    pltpu.make_async_copy(hall.at[0, 0:31], hall.at[0, 0:31], tap_s).wait()
    pltpu.make_async_copy(hall.at[0:3], hall.at[0:3], gat_s).wait()
    for ch in range(CI):
        await_all(sendu, ch, CI, u_s)
        await_all(sendd, ch, CI, d_s)
    for ch in range(CO):
        await_all(sendz, ch, CO, z_s)
        await_all(sendi, ch, CO, i_s)
    pltpu.make_async_copy(dfs.at[0:3], dfs.at[0:3], df_s).wait()
    swap_df.wait_send()


def local(grad_out, saved_input, gate_value, filter_taps, skip_gain, lang_ids, doc_ids, dro_weight):
    vmem = pl.BlockSpec(memory_space=pltpu.VMEM)
    dma = pltpu.SemaphoreType.DMA
    token = jax.ShapeDtypeStruct((1, 128, 2048), BF)
    return pl.pallas_call(
        kernel,
        out_shape=(token, token, jax.ShapeDtypeStruct((64, 512), F32)),
        in_specs=[vmem] * 7 + [pl.BlockSpec(memory_space=pltpu.SMEM)] + [vmem] * 6,
        out_specs=(vmem, vmem, vmem),
        scratch_shapes=[
            pltpu.VMEM((1, 128), jnp.int32),
            pltpu.VMEM((NCTX, 1, 128), jnp.int32),
            pltpu.VMEM((NX, NCTX, 16, 128), BF),
            pltpu.VMEM((4, NCTX, 16, 128), BF),
            pltpu.VMEM((128, 128), F32),
            pltpu.VMEM((32, 256, 256), BF),
            pltpu.VMEM((32, 256, 256), BF),
            pltpu.VMEM((1024, 512), BF),
            pltpu.VMEM((512, 1024), BF),
            *[pltpu.VMEM((4, NCTX, 16, 128), BF)] * 8,
            pltpu.VMEM((32, 2, GR, 16, 128), BF),
            pltpu.VMEM((4, 32, 2, 16, 128), BF),
            pltpu.VMEM((4, 32, 2, 16, 128), BF),
            pltpu.VMEM((32, 256, 128), F32),
            pltpu.VMEM((32, 256, 128), F32),
            pltpu.VMEM((32, 256, 128), F32),
            pltpu.VMEM((NX, 2, 4, 4, 16, 128), BF),
            pltpu.VMEM((NX, 2, 4, 4, 16, 128), BF),
            pltpu.VMEM((4, 4, 16, 128), BF),
            pltpu.VMEM((4, 4, 16, 128), BF),
            dma, dma, dma, dma, dma, dma,
            *[dma((CI,))] * 4,
            *[dma((CO,))] * 4,
            dma, dma, dma, dma, dma((5,)),
        ],
        compiler_params=pltpu.CompilerParams(
            collective_id=0, has_side_effects=True, vmem_limit_bytes=56 << 20
        ),
        name="hyena_backward",
    )(
        grad_out, saved_input, gate_value, filter_taps, skip_gain.reshape(16, 128), lang_ids, doc_ids, dro_weight,
        *tables(),
    )


def solution(mesh):
    return jax.shard_map(
        local,
        mesh=mesh,
        in_specs=(
            P("dp", "ctx", None), P("dp", "ctx", None), P("dp", "ctx", None), P(None, "ctx"),
            P(), P("dp", "ctx"), P("dp", "ctx"), P(),
        ),
        out_specs=(P("dp", "ctx", None), P("dp", "ctx", None), P("ctx", "dp")),
        check_vma=False,
    )
```

```python
import functools
import math

import jax
import jax.numpy as jnp
import numpy as np
from jax import lax
from jax.experimental import pallas as pl
from jax.experimental.pallas import tpu as pltpu
from jax.sharding import PartitionSpec as P

MESH = pl.DeviceIdType.MESH
BF = jnp.bfloat16
F32 = jnp.float32
NCTX, NDP, NX = 32, 8, 4
LEN = 4096
CC = (2, 2)
FIRST = 1
GR = 8
CI, CO = CC
UN = 8


def tables():
    k1 = np.arange(32)
    a = np.arange(32)
    b = np.arange(128)
    phi = 2 * math.pi / 128 * ((a[None, :] * (4 * k1[:, None] + 1)) % 128)
    first = np.zeros((64, 128), np.float32)
    first[:, :32] = np.stack([np.cos(phi), -np.sin(phi)], 1).reshape(64, 32)
    last = np.zeros((32, 128), np.float32)
    last[:, :64] = first[:, :32].T / LEN
    alpha = 2 * math.pi / 16384 * ((b[None, :] * (4 * k1[:, None] + 1)) % 16384)
    beta = 2 * math.pi / 128 * ((b[None, :] * b[:, None]) % 128)
    f = lambda v: jnp.asarray(v.astype(np.float32))
    return (
        jnp.asarray(first, BF),
        jnp.asarray(last, BF),
        f(np.cos(alpha)),
        f(np.sin(alpha)),
        f(np.cos(beta)),
        f(np.sin(beta)),
    )


def iota(shape, dim):
    return lax.broadcasted_iota(jnp.int32, shape, dim)


def swap(x):
    return pltpu.roll(x, 64, axis=1)


def kernel(
    grad, sig, gate, taps, skip, lang, docs, dro, first, last, cosa, sina, cosb, sinb,
    d_input, d_gate, d_filter,
    docs_out, docs_all, hall, htime, scale, mats, matst, fone, ftwo, sendu, recvu, sendd, recvd, sendz, recvz,
    sendi, recvi, ybuf, vbuf, qbuf, hspec, uspec, gspec, dfs, dfr, dft, dfq,
    doc_s, doc_r, tap_s, tap_r, gat_s, gat_r, u_s, u_r, d_s, d_r, z_s, z_r, i_s, i_r, df_s, df_r, dq_s, dq_r, own,
):
    me = lax.axis_index("ctx")
    dp = lax.axis_index("dp")
    xs = lax.rem(dp, NX)
    zl = dp // NX
    low = iota((16, 128), 1) < 64

    def peer_of(p):
        return lax.rem(me + p, NCTX)

    def x_of(q):
        return zl * NX + lax.rem(xs + q, NX)

    barrier = pltpu.get_barrier_semaphore()

    @pl.loop(1, NCTX)
    def _(p):
        pl.semaphore_signal(barrier, inc=1, device_id={"ctx": peer_of(p)}, device_id_type=MESH)

    across = lax.rem(dp + NX, NDP)

    @pl.loop(1, NX)
    def _(q):
        pl.semaphore_signal(barrier, inc=1, device_id={"dp": x_of(q)}, device_id_type=MESH)

    pl.semaphore_signal(barrier, inc=1, device_id={"dp": across}, device_id_type=MESH)

    def pair_store(dst, g, m, first_half, second_half):
        dst[g, 2 * m] = jnp.where(low, first_half, swap(second_half)).astype(BF)
        dst[g, 2 * m + 1] = jnp.where(low, swap(first_half), second_half).astype(BF)

    def rows_of(g):
        return pl.ds(pl.multiple_of(16 * g, 16), 16)

    docs_row = docs[...]
    docs_out[...] = docs_row
    docs_all[me] = docs_row

    pl.semaphore_wait(barrier, NCTX - 1 + NX)

    @pl.loop(1, NCTX)
    def _(p):
        peer = peer_of(p)
        pltpu.make_async_remote_copy(
            docs_out, docs_all.at[me], doc_s, doc_r, device_id={"ctx": peer}, device_id_type=MESH
        ).start()

    def tap_rows(j):
        return taps.at[pl.ds(pl.multiple_of(64 * j + 16 * xs, 16), 16), :]

    @pl.loop(1, NCTX)
    def _(p):
        peer = peer_of(p)
        pltpu.make_async_remote_copy(
            tap_rows(peer), hall.at[xs, me], tap_s, tap_r, device_id={"ctx": peer}, device_id_type=MESH
        ).start()

    own_taps = pltpu.make_async_copy(tap_rows(me), hall.at[xs, me], own.at[0])
    own_taps.start()

    def send_part(src, dst, span, sems, semr):
        @pl.loop(1, NCTX)
        def _(p):
            peer = peer_of(p)
            pltpu.make_async_remote_copy(
                src.at[span, peer], dst.at[span, me], sems, semr,
                device_id={"ctx": peer}, device_id_type=MESH,
            ).start()

    def spread(src, dst, chunk, chunks, sems, semr):
        per = src.shape[0] // chunks
        send_part(src, dst, slice(per * chunk, per * chunk + per), sems.at[chunk], semr.at[chunk])

    def await_all(buf, chunk, chunks, sem):
        per = buf.shape[0] // chunks
        part = buf.at[per * chunk:per * chunk + per, 0:31]
        pltpu.make_async_copy(part, part, sem.at[chunk]).wait()

    @pl.loop(0, 4)
    def _(g):
        for m in range(16):
            cols = slice(128 * m, 128 * m + 128)
            pair_store(sendu, g, m, sig[0, rows_of(g), cols].astype(F32), sig[0, rows_of(g + 4), cols].astype(F32))

    send_part(sendu, recvu, slice(0, 1), u_s.at[0], u_r.at[0])

    own_taps.wait()
    pltpu.make_async_copy(hall.at[0, 0:31], hall.at[0, 0:31], tap_r).wait()

    @pl.loop(1, NX)
    def _(q):
        pltpu.make_async_remote_copy(
            hall.at[xs], hall.at[xs], gat_s, gat_r, device_id={"dp": x_of(q)}, device_id_type=MESH
        ).start()

    send_part(sendu, recvu, slice(1, 4), u_s.at[1], u_r.at[1])

    def column(row):
        return jnp.broadcast_to(row.astype(F32), (128, 128)).T

    own_docs = column(docs_row)
    own_lang = column(lang[...])
    weight = jnp.zeros((128, 128), F32)
    for group in range(16):
        weight = jnp.where(own_lang == float(group), dro[group], weight)
    pltpu.make_async_copy(docs_all.at[0:31], docs_all.at[0:31], doc_r).wait()

    def count(a, total):
        row = jnp.broadcast_to(docs_all[a].astype(F32), (128, 128))
        return total + jnp.where(row == own_docs, 1.0, 0.0)

    hits = lax.fori_loop(0, NCTX, count, jnp.zeros((128, 128), F32))
    doc_len = jnp.sum(hits, axis=1, keepdims=True)
    scale[...] = weight * 256.0 / (doc_len + 128.0)

    for ch in range(CI):
        @pl.loop(4 // CI * ch, 4 // CI * ch + 4 // CI)
        def _(g):
            for m in range(16):
                cols = slice(128 * m, 128 * m + 128)
                halves = []
                for h in range(2):
                    rows = rows_of(g + 4 * h)
                    dy = grad[0, rows, cols].astype(F32) * scale[rows, :]
                    halves.append(dy * gate[0, rows, cols].astype(F32))
                pair_store(sendd, g, m, *halves)

        spread(sendd, recvd, ch, CI, d_s, d_r)

    own_u = pltpu.make_async_copy(sendu.at[:, me], recvu.at[:, me], own.at[1])
    own_u.start()
    own_d = pltpu.make_async_copy(sendd.at[:, me], recvd.at[:, me], own.at[4])
    own_d.start()

    def expand(small, rows, cols):
        left = (iota((rows, small.shape[0]), 0) // 16 == iota((rows, small.shape[0]), 1)).astype(F32).astype(BF)
        right = (iota((128, cols), 1) // 16 == iota((128, cols), 0)).astype(F32).astype(BF)
        tall = jnp.dot(left, small, preferred_element_type=F32).astype(BF)
        wide = jnp.dot(tall, right, preferred_element_type=F32)
        keep = lax.rem(iota((rows, cols), 0), 16) == lax.rem(iota((rows, cols), 1), 16)
        return jnp.where(keep, wide, 0.0).astype(BF)

    fone[...] = expand(first[...], 1024, 512)
    ftwo[...] = expand(last[...], 512, 1024)

    @pl.loop(0, 32, unroll=2)
    def _(k):
        ca, sa = cosa[pl.ds(k, 1), :], sina[pl.ds(k, 1), :]
        co = ca * cosb[...] - sa * sinb[...]
        si = sa * cosb[...] + ca * sinb[...]
        mats[k, 0:128, 0:128] = co.astype(BF)
        mats[k, 0:128, 128:256] = si.astype(BF)
        mats[k, 128:256, 0:128] = (-si).astype(BF)
        mats[k, 128:256, 128:256] = co.astype(BF)
        cot, sit = co.T, si.T
        matst[k, 0:128, 0:128] = cot.astype(BF)
        matst[k, 0:128, 128:256] = (-sit).astype(BF)
        matst[k, 128:256, 0:128] = sit.astype(BF)
        matst[k, 128:256, 128:256] = cot.astype(BF)

    def stage_one(x, g, lanes):
        y = jnp.dot(fone[...], x.reshape(512, 128), preferred_element_type=F32)
        ybuf[:, :, g, :, 0:lanes] = y[:, 0:lanes].astype(BF).reshape(32, 2, 16, lanes)
        ybuf[:, :, g + 4, :, 0:lanes] = swap(y)[:, 0:lanes].astype(BF).reshape(32, 2, 16, lanes)

    def stage_two(k):
        return jnp.dot(mats[k], ybuf[k].reshape(256, 128), preferred_element_type=F32)

    pltpu.make_async_copy(hall.at[0:3], hall.at[0:3], gat_r).wait()

    @pl.loop(0, NCTX, unroll=4)
    def _(a):
        block = hall[:, a].reshape(64, 128).astype(F32)
        turned = jnp.concatenate([swap(block), block], axis=0).T
        htime[:, a] = turned[0:64].astype(BF).reshape(4, 16, 128)

    @pl.loop(0, 4)
    def _(g):
        stage_one(htime[g], g, 128)

    gain = skip[pl.ds(me // 2, 1), :]
    turned_gain = pltpu.roll(jnp.broadcast_to(gain, (8, 128)), 64, axis=1)[0:1]
    low_row = iota((1, 128), 1) < 64
    even = jnp.where(low_row, gain, turned_gain)
    odd = jnp.where(low_row, turned_gain, gain)
    parity = lax.rem(me, 2).astype(F32)
    gain2 = even * (1.0 - parity) + odd * parity
    half_low = iota((64, 128), 1) < 64

    def invert(k, p, buf):
        v = jnp.dot(matst[k], p.astype(BF), preferred_element_type=F32).reshape(2, 2, 64, 128)
        for c in range(2):
            both = jnp.where(half_low, v[c, 0], swap(v[c, 1]))
            buf[:, k, c] = both.astype(BF).reshape(4, 16, 128)

    def bring(recv, local_copy, sem, spans):
        local_copy.wait()
        for ch, (start, stop) in enumerate(spans):
            part = recv.at[start:stop, 0:31]
            pltpu.make_async_copy(part, part, sem.at[ch]).wait()

            @pl.loop(start, stop)
            def _(g):
                stage_one(recv[g], g, 64)

    def send_back(source, send, recv, chunks, sems, semr):
        for ch in chunks:
            @pl.loop(4 // CO * ch, 4 // CO * ch + 4 // CO)
            def _(g):
                o = jnp.dot(ftwo[...], vbuf[g].reshape(1024, 128), preferred_element_type=F32)
                o = o + gain2 * source[g].reshape(512, 128).astype(F32)
                send[g] = o.astype(BF).reshape(32, 16, 128)

            spread(send, recv, ch, CO, sems, semr)

    bring(recvu, own_u, u_r, ((0, 1), (1, 4)))

    @pl.loop(0, 32, unroll=UN)
    def _(k):
        s = stage_two(k)
        uspec[k] = s
        h = swap(s)
        hspec[k] = h
        sr, si = s[0:128], s[128:256]
        hr, hi = h[0:128], h[128:256]
        invert(k, jnp.concatenate([sr * hr - si * hi, sr * hi + si * hr], axis=0), vbuf)

    send_back(recvu, sendz, recvz, range(CO), z_s, z_r)
    own_z = pltpu.make_async_copy(sendz.at[:, me], recvz.at[:, me], own.at[2])
    own_z.start()

    bring(recvd, own_d, d_r, ((0, 2), (2, 4)))

    @pl.loop(0, 32, unroll=UN)
    def _(k):
        s = stage_two(k)
        gspec[k] = s
        sr, si = s[0:128], s[128:256]
        hr, hi = hspec[k, 0:128], hspec[k, 128:256]
        invert(k, jnp.concatenate([sr * hr + si * hi, si * hr - sr * hi], axis=0), vbuf)

    send_back(recvd, sendi, recvi, range(FIRST), i_s, i_r)

    @pl.loop(0, 32, unroll=UN)
    def _(k):
        sr, si = gspec[k, 0:128], gspec[k, 128:256]
        ur, ui = uspec[k, 0:128], uspec[k, 128:256]
        invert(k, jnp.concatenate([sr * ur + si * ui, si * ur - sr * ui], axis=0), qbuf)

    @pl.loop(0, 4)
    def _(g):
        o = jnp.dot(ftwo[...], qbuf[g].reshape(1024, 128), preferred_element_type=F32)
        o = o.astype(BF).reshape(2, 4, 4, 16, 128)
        dfs[:, 0, g] = o[0]
        dfs[:, 1, g] = o[1]

    @pl.loop(1, NX)
    def _(q):
        other = lax.rem(xs + q, NX)
        pltpu.make_async_remote_copy(
            dfs.at[other], dfr.at[xs], df_s, df_r, device_id={"dp": x_of(q)}, device_id_type=MESH
        ).start()

    own_df = pltpu.make_async_copy(dfs.at[xs], dfr.at[xs], own.at[3])
    own_df.start()
    send_back(recvd, sendi, recvi, range(FIRST, CO), i_s, i_r)
    own_i = pltpu.make_async_copy(sendi.at[:, me], recvi.at[:, me], own.at[0])
    own_i.start()

    own_df.wait()
    pltpu.make_async_copy(dfr.at[0:3], dfr.at[0:3], df_r).wait()

    def x_sum(zside):
        total = dfr[0, zside].astype(F32)
        for r in range(1, NX):
            total = total + dfr[r, zside].astype(F32)
        return total

    dft[...] = x_sum(1 - zl).astype(BF)
    swap_df = pltpu.make_async_remote_copy(
        dft, dfq, dq_s, dq_r, device_id={"dp": across}, device_id_type=MESH
    )
    swap_df.start()
    own_z.wait()
    own_i.wait()

    def unpair(recv, g, m):
        left, right = recv[g, 2 * m].astype(F32), recv[g, 2 * m + 1].astype(F32)
        return jnp.where(low, left, swap(right)), jnp.where(low, swap(left), right)

    for ch in range(CO):
        await_all(recvz, ch, CO, z_r)

        @pl.loop(4 // CO * ch, 4 // CO * ch + 4 // CO)
        def _(g):
            for m in range(16):
                cols = slice(128 * m, 128 * m + 128)
                for h, z in enumerate(unpair(recvz, g, m)):
                    rows = rows_of(g + 4 * h)
                    d_gate[0, rows, cols] = (grad[0, rows, cols].astype(F32) * scale[rows, :] * z).astype(BF)

    for ch in range(CO):
        await_all(recvi, ch, CO, i_r)

        @pl.loop(4 // CO * ch, 4 // CO * ch + 4 // CO)
        def _(g):
            for m in range(16):
                cols = slice(128 * m, 128 * m + 128)
                for h, v in enumerate(unpair(recvi, g, m)):
                    d_input[0, rows_of(g + 4 * h), cols] = v.astype(BF)

    swap_df.wait_recv()
    final = x_sum(zl) + dfq[...].astype(F32)
    for a in range(4):
        turned = final[:, a].reshape(64, 128).T
        d_filter[:, 128 * a:128 * a + 64] = turned[0:64]
        d_filter[:, 128 * a + 64:128 * a + 128] = turned[64:128]

    pltpu.make_async_copy(docs_all.at[0:31], docs_all.at[0:31], doc_s).wait()
    pltpu.make_async_copy(hall.at[0, 0:31], hall.at[0, 0:31], tap_s).wait()
    pltpu.make_async_copy(hall.at[0:3], hall.at[0:3], gat_s).wait()
    for ch, (start, stop) in enumerate(((0, 1), (1, 4))):
        part = sendu.at[start:stop, 0:31]
        pltpu.make_async_copy(part, part, u_s.at[ch]).wait()
    for ch in range(CI):
        await_all(sendd, ch, CI, d_s)
    for ch in range(CO):
        await_all(sendz, ch, CO, z_s)
        await_all(sendi, ch, CO, i_s)
    pltpu.make_async_copy(dfs.at[0:3], dfs.at[0:3], df_s).wait()
    swap_df.wait_send()


def local(grad_out, saved_input, gate_value, filter_taps, skip_gain, lang_ids, doc_ids, dro_weight):
    vmem = pl.BlockSpec(memory_space=pltpu.VMEM)
    dma = pltpu.SemaphoreType.DMA
    token = jax.ShapeDtypeStruct((1, 128, 2048), BF)
    return pl.pallas_call(
        kernel,
        out_shape=(token, token, jax.ShapeDtypeStruct((64, 512), F32)),
        in_specs=[vmem] * 7 + [pl.BlockSpec(memory_space=pltpu.SMEM)] + [vmem] * 6,
        out_specs=(vmem, vmem, vmem),
        scratch_shapes=[
            pltpu.VMEM((1, 128), jnp.int32),
            pltpu.VMEM((NCTX, 1, 128), jnp.int32),
            pltpu.VMEM((NX, NCTX, 16, 128), BF),
            pltpu.VMEM((4, NCTX, 16, 128), BF),
            pltpu.VMEM((128, 128), F32),
            pltpu.VMEM((32, 256, 256), BF),
            pltpu.VMEM((32, 256, 256), BF),
            pltpu.VMEM((1024, 512), BF),
            pltpu.VMEM((512, 1024), BF),
            *[pltpu.VMEM((4, NCTX, 16, 128), BF)] * 8,
            pltpu.VMEM((32, 2, GR, 16, 128), BF),
            pltpu.VMEM((4, 32, 2, 16, 128), BF),
            pltpu.VMEM((4, 32, 2, 16, 128), BF),
            pltpu.VMEM((32, 256, 128), F32),
            pltpu.VMEM((32, 256, 128), F32),
            pltpu.VMEM((32, 256, 128), F32),
            pltpu.VMEM((NX, 2, 4, 4, 16, 128), BF),
            pltpu.VMEM((NX, 2, 4, 4, 16, 128), BF),
            pltpu.VMEM((4, 4, 16, 128), BF),
            pltpu.VMEM((4, 4, 16, 128), BF),
            dma, dma, dma, dma, dma, dma,
            *[dma((CI,))] * 4,
            *[dma((CO,))] * 4,
            dma, dma, dma, dma, dma((5,)),
        ],
        compiler_params=pltpu.CompilerParams(
            collective_id=0, has_side_effects=True, vmem_limit_bytes=56 << 20
        ),
        name="hyena_backward",
    )(
        grad_out, saved_input, gate_value, filter_taps, skip_gain.reshape(16, 128), lang_ids, doc_ids, dro_weight,
        *tables(),
    )


def solution(mesh):
    return jax.shard_map(
        local,
        mesh=mesh,
        in_specs=(
            P("dp", "ctx", None), P("dp", "ctx", None), P("dp", "ctx", None), P(None, "ctx"),
            P(), P("dp", "ctx"), P("dp", "ctx"), P(),
        ),
        out_specs=(P("dp", "ctx", None), P("dp", "ctx", None), P("ctx", "dp")),
        check_vma=False,
    )
```

```python
import functools
import math

import jax
import jax.numpy as jnp
import numpy as np
from jax import lax
from jax.experimental import pallas as pl
from jax.experimental.pallas import tpu as pltpu
from jax.sharding import PartitionSpec as P

MESH = pl.DeviceIdType.MESH
BF = jnp.bfloat16
F32 = jnp.float32
NCTX, NDP, NX = 32, 8, 4
LEN = 4096
CC = (2, 2)
FIRST = 1
GR = 8
CI, CO = CC
UN = 8
US = 31


def tables():
    k1 = np.arange(32)
    a = np.arange(32)
    b = np.arange(128)
    phi = 2 * math.pi / 128 * ((a[None, :] * (4 * k1[:, None] + 1)) % 128)
    first = np.zeros((64, 128), np.float32)
    first[:, :32] = np.stack([np.cos(phi), -np.sin(phi)], 1).reshape(64, 32)
    last = np.zeros((32, 128), np.float32)
    last[:, :64] = first[:, :32].T / LEN
    alpha = 2 * math.pi / 16384 * ((b[None, :] * (4 * k1[:, None] + 1)) % 16384)
    beta = 2 * math.pi / 128 * ((b[None, :] * b[:, None]) % 128)
    f = lambda v: jnp.asarray(v.astype(np.float32))
    return (
        jnp.asarray(first, BF),
        jnp.asarray(last, BF),
        f(np.cos(alpha)),
        f(np.sin(alpha)),
        f(np.cos(beta)),
        f(np.sin(beta)),
    )


def iota(shape, dim):
    return lax.broadcasted_iota(jnp.int32, shape, dim)


def swap(x):
    return pltpu.roll(x, 64, axis=1)


def kernel(
    grad_hbm, sig_hbm, gate_hbm, taps, skip, lang, docs, dro, first, last, cosa, sina, cosb, sinb,
    d_input, d_gate, d_filter,
    grad, sig, gate, stage, docs_out, docs_all, hall, htime, scale, mats, matst, fone, ftwo, sendu, recvu, sendd, recvd, sendz, recvz,
    sendi, recvi, ybuf, vbuf, qbuf, hspec, uspec, gspec, dfs, dfr, dft, dfq,
    doc_s, doc_r, tap_s, tap_r, gat_s, gat_r, u_s, u_r, d_s, d_r, z_s, z_r, i_s, i_r, df_s, df_r, dq_s, dq_r, own,
):
    me = lax.axis_index("ctx")
    dp = lax.axis_index("dp")
    xs = lax.rem(dp, NX)
    zl = dp // NX
    low = iota((16, 128), 1) < 64

    def peer_of(p):
        return lax.rem(me + p, NCTX)

    def x_of(q):
        return zl * NX + lax.rem(xs + q, NX)

    staged = [
        pltpu.make_async_copy(src, dst, stage.at[i])
        for i, (src, dst) in enumerate(((sig_hbm, sig), (grad_hbm, grad), (gate_hbm, gate)))
    ]
    for copy in staged:
        copy.start()
    barrier = pltpu.get_barrier_semaphore()

    @pl.loop(1, NCTX)
    def _(p):
        pl.semaphore_signal(barrier, inc=1, device_id={"ctx": peer_of(p)}, device_id_type=MESH)

    across = lax.rem(dp + NX, NDP)

    @pl.loop(1, NX)
    def _(q):
        pl.semaphore_signal(barrier, inc=1, device_id={"dp": x_of(q)}, device_id_type=MESH)

    pl.semaphore_signal(barrier, inc=1, device_id={"dp": across}, device_id_type=MESH)

    def pair_store(dst, g, m, first_half, second_half):
        dst[g, 2 * m] = jnp.where(low, first_half, swap(second_half)).astype(BF)
        dst[g, 2 * m + 1] = jnp.where(low, swap(first_half), second_half).astype(BF)

    def rows_of(g):
        return pl.ds(pl.multiple_of(16 * g, 16), 16)

    docs_row = docs[...]
    docs_out[...] = docs_row
    docs_all[me] = docs_row

    pl.semaphore_wait(barrier, NCTX - 1 + NX)

    @pl.loop(1, NCTX)
    def _(p):
        peer = peer_of(p)
        pltpu.make_async_remote_copy(
            docs_out, docs_all.at[me], doc_s, doc_r, device_id={"ctx": peer}, device_id_type=MESH
        ).start()

    def tap_rows(j):
        return taps.at[pl.ds(pl.multiple_of(64 * j + 16 * xs, 16), 16), :]

    @pl.loop(1, NCTX)
    def _(p):
        peer = peer_of(p)
        pltpu.make_async_remote_copy(
            tap_rows(peer), hall.at[xs, me], tap_s, tap_r, device_id={"ctx": peer}, device_id_type=MESH
        ).start()

    own_taps = pltpu.make_async_copy(tap_rows(me), hall.at[xs, me], own.at[0])
    own_taps.start()

    def send_part(src, dst, span, sems, semr):
        @pl.loop(1, NCTX, unroll=US)
        def _(p):
            peer = peer_of(p)
            pltpu.make_async_remote_copy(
                src.at[span, peer], dst.at[span, me], sems, semr,
                device_id={"ctx": peer}, device_id_type=MESH,
            ).start()

    def spread(src, dst, chunk, chunks, sems, semr):
        per = src.shape[0] // chunks
        send_part(src, dst, slice(per * chunk, per * chunk + per), sems.at[chunk], semr.at[chunk])

    def await_all(buf, chunk, chunks, sem):
        per = buf.shape[0] // chunks
        part = buf.at[per * chunk:per * chunk + per, 0:31]
        pltpu.make_async_copy(part, part, sem.at[chunk]).wait()

    staged[0].wait()

    @pl.loop(0, 4)
    def _(g):
        for m in range(16):
            cols = slice(128 * m, 128 * m + 128)
            pair_store(sendu, g, m, sig[0, rows_of(g), cols].astype(F32), sig[0, rows_of(g + 4), cols].astype(F32))

    send_part(sendu, recvu, slice(0, 1), u_s.at[0], u_r.at[0])

    own_taps.wait()
    pltpu.make_async_copy(hall.at[0, 0:31], hall.at[0, 0:31], tap_r).wait()

    @pl.loop(1, NX)
    def _(q):
        pltpu.make_async_remote_copy(
            hall.at[xs], hall.at[xs], gat_s, gat_r, device_id={"dp": x_of(q)}, device_id_type=MESH
        ).start()

    send_part(sendu, recvu, slice(1, 4), u_s.at[1], u_r.at[1])

    staged[1].wait()
    staged[2].wait()

    def column(row):
        return jnp.broadcast_to(row.astype(F32), (128, 128)).T

    own_docs = column(docs_row)
    own_lang = column(lang[...])
    weight = jnp.zeros((128, 128), F32)
    for group in range(16):
        weight = jnp.where(own_lang == float(group), dro[group], weight)
    pltpu.make_async_copy(docs_all.at[0:31], docs_all.at[0:31], doc_r).wait()

    def count(a, total):
        row = jnp.broadcast_to(docs_all[a].astype(F32), (128, 128))
        return total + jnp.where(row == own_docs, 1.0, 0.0)

    hits = lax.fori_loop(0, NCTX, count, jnp.zeros((128, 128), F32))
    doc_len = jnp.sum(hits, axis=1, keepdims=True)
    scale[...] = weight * 256.0 / (doc_len + 128.0)

    for ch in range(CI):
        @pl.loop(4 // CI * ch, 4 // CI * ch + 4 // CI)
        def _(g):
            for m in range(16):
                cols = slice(128 * m, 128 * m + 128)
                halves = []
                for h in range(2):
                    rows = rows_of(g + 4 * h)
                    dy = grad[0, rows, cols].astype(F32) * scale[rows, :]
                    halves.append(dy * gate[0, rows, cols].astype(F32))
                pair_store(sendd, g, m, *halves)

        spread(sendd, recvd, ch, CI, d_s, d_r)

    own_u = pltpu.make_async_copy(sendu.at[:, me], recvu.at[:, me], own.at[1])
    own_u.start()
    own_d = pltpu.make_async_copy(sendd.at[:, me], recvd.at[:, me], own.at[4])
    own_d.start()

    def expand(small, rows, cols):
        left = (iota((rows, small.shape[0]), 0) // 16 == iota((rows, small.shape[0]), 1)).astype(F32).astype(BF)
        right = (iota((128, cols), 1) // 16 == iota((128, cols), 0)).astype(F32).astype(BF)
        tall = jnp.dot(left, small, preferred_element_type=F32).astype(BF)
        wide = jnp.dot(tall, right, preferred_element_type=F32)
        keep = lax.rem(iota((rows, cols), 0), 16) == lax.rem(iota((rows, cols), 1), 16)
        return jnp.where(keep, wide, 0.0).astype(BF)

    fone[...] = expand(first[...], 1024, 512)
    ftwo[...] = expand(last[...], 512, 1024)

    @pl.loop(0, 32, unroll=2)
    def _(k):
        ca, sa = cosa[pl.ds(k, 1), :], sina[pl.ds(k, 1), :]
        co = ca * cosb[...] - sa * sinb[...]
        si = sa * cosb[...] + ca * sinb[...]
        mats[k, 0:128, 0:128] = co.astype(BF)
        mats[k, 0:128, 128:256] = si.astype(BF)
        mats[k, 128:256, 0:128] = (-si).astype(BF)
        mats[k, 128:256, 128:256] = co.astype(BF)
        cot, sit = co.T, si.T
        matst[k, 0:128, 0:128] = cot.astype(BF)
        matst[k, 0:128, 128:256] = (-sit).astype(BF)
        matst[k, 128:256, 0:128] = sit.astype(BF)
        matst[k, 128:256, 128:256] = cot.astype(BF)

    def stage_one(x, g, lanes):
        y = jnp.dot(fone[...], x.reshape(512, 128), preferred_element_type=F32)
        ybuf[:, :, g, :, 0:lanes] = y[:, 0:lanes].astype(BF).reshape(32, 2, 16, lanes)
        ybuf[:, :, g + 4, :, 0:lanes] = swap(y)[:, 0:lanes].astype(BF).reshape(32, 2, 16, lanes)

    def stage_two(k):
        return jnp.dot(mats[k], ybuf[k].reshape(256, 128), preferred_element_type=F32)

    pltpu.make_async_copy(hall.at[0:3], hall.at[0:3], gat_r).wait()

    @pl.loop(0, NCTX, unroll=4)
    def _(a):
        block = hall[:, a].reshape(64, 128).astype(F32)
        turned = jnp.concatenate([swap(block), block], axis=0).T
        htime[:, a] = turned[0:64].astype(BF).reshape(4, 16, 128)

    @pl.loop(0, 4)
    def _(g):
        stage_one(htime[g], g, 128)

    gain = skip[pl.ds(me // 2, 1), :]
    turned_gain = pltpu.roll(jnp.broadcast_to(gain, (8, 128)), 64, axis=1)[0:1]
    low_row = iota((1, 128), 1) < 64
    even = jnp.where(low_row, gain, turned_gain)
    odd = jnp.where(low_row, turned_gain, gain)
    parity = lax.rem(me, 2).astype(F32)
    gain2 = even * (1.0 - parity) + odd * parity
    half_low = iota((64, 128), 1) < 64

    def invert(k, p, buf):
        v = jnp.dot(matst[k], p.astype(BF), preferred_element_type=F32).reshape(2, 2, 64, 128)
        for c in range(2):
            both = jnp.where(half_low, v[c, 0], swap(v[c, 1]))
            buf[:, k, c] = both.astype(BF).reshape(4, 16, 128)

    def bring(recv, local_copy, sem, spans):
        local_copy.wait()
        for ch, (start, stop) in enumerate(spans):
            part = recv.at[start:stop, 0:31]
            pltpu.make_async_copy(part, part, sem.at[ch]).wait()

            @pl.loop(start, stop)
            def _(g):
                stage_one(recv[g], g, 64)

    def send_back(source, send, recv, chunks, sems, semr):
        for ch in chunks:
            @pl.loop(4 // CO * ch, 4 // CO * ch + 4 // CO)
            def _(g):
                o = jnp.dot(ftwo[...], vbuf[g].reshape(1024, 128), preferred_element_type=F32)
                o = o + gain2 * source[g].reshape(512, 128).astype(F32)
                send[g] = o.astype(BF).reshape(32, 16, 128)

            spread(send, recv, ch, CO, sems, semr)

    bring(recvu, own_u, u_r, ((0, 1), (1, 4)))

    @pl.loop(0, 32, unroll=UN)
    def _(k):
        s = stage_two(k)
        uspec[k] = s
        h = swap(s)
        hspec[k] = h
        sr, si = s[0:128], s[128:256]
        hr, hi = h[0:128], h[128:256]
        invert(k, jnp.concatenate([sr * hr - si * hi, sr * hi + si * hr], axis=0), vbuf)

    send_back(recvu, sendz, recvz, range(CO), z_s, z_r)
    own_z = pltpu.make_async_copy(sendz.at[:, me], recvz.at[:, me], own.at[2])
    own_z.start()

    bring(recvd, own_d, d_r, ((0, 2), (2, 4)))

    @pl.loop(0, 32, unroll=UN)
    def _(k):
        s = stage_two(k)
        gspec[k] = s
        sr, si = s[0:128], s[128:256]
        hr, hi = hspec[k, 0:128], hspec[k, 128:256]
        invert(k, jnp.concatenate([sr * hr + si * hi, si * hr - sr * hi], axis=0), vbuf)

    send_back(recvd, sendi, recvi, range(FIRST), i_s, i_r)

    @pl.loop(0, 32, unroll=UN)
    def _(k):
        sr, si = gspec[k, 0:128], gspec[k, 128:256]
        ur, ui = uspec[k, 0:128], uspec[k, 128:256]
        invert(k, jnp.concatenate([sr * ur + si * ui, si * ur - sr * ui], axis=0), qbuf)

    @pl.loop(0, 4)
    def _(g):
        o = jnp.dot(ftwo[...], qbuf[g].reshape(1024, 128), preferred_element_type=F32)
        o = o.astype(BF).reshape(2, 4, 4, 16, 128)
        dfs[:, 0, g] = o[0]
        dfs[:, 1, g] = o[1]

    @pl.loop(1, NX)
    def _(q):
        other = lax.rem(xs + q, NX)
        pltpu.make_async_remote_copy(
            dfs.at[other], dfr.at[xs], df_s, df_r, device_id={"dp": x_of(q)}, device_id_type=MESH
        ).start()

    own_df = pltpu.make_async_copy(dfs.at[xs], dfr.at[xs], own.at[3])
    own_df.start()
    send_back(recvd, sendi, recvi, range(FIRST, CO), i_s, i_r)
    own_i = pltpu.make_async_copy(sendi.at[:, me], recvi.at[:, me], own.at[0])
    own_i.start()

    own_df.wait()
    pltpu.make_async_copy(dfr.at[0:3], dfr.at[0:3], df_r).wait()

    def x_sum(zside):
        total = dfr[0, zside].astype(F32)
        for r in range(1, NX):
            total = total + dfr[r, zside].astype(F32)
        return total

    dft[...] = x_sum(1 - zl).astype(BF)
    swap_df = pltpu.make_async_remote_copy(
        dft, dfq, dq_s, dq_r, device_id={"dp": across}, device_id_type=MESH
    )
    swap_df.start()
    own_z.wait()
    own_i.wait()

    def unpair(recv, g, m):
        left, right = recv[g, 2 * m].astype(F32), recv[g, 2 * m + 1].astype(F32)
        return jnp.where(low, left, swap(right)), jnp.where(low, swap(left), right)

    for ch in range(CO):
        await_all(recvz, ch, CO, z_r)

        @pl.loop(4 // CO * ch, 4 // CO * ch + 4 // CO)
        def _(g):
            for m in range(16):
                cols = slice(128 * m, 128 * m + 128)
                for h, z in enumerate(unpair(recvz, g, m)):
                    rows = rows_of(g + 4 * h)
                    d_gate[0, rows, cols] = (grad[0, rows, cols].astype(F32) * scale[rows, :] * z).astype(BF)

    for ch in range(CO):
        await_all(recvi, ch, CO, i_r)

        @pl.loop(4 // CO * ch, 4 // CO * ch + 4 // CO)
        def _(g):
            for m in range(16):
                cols = slice(128 * m, 128 * m + 128)
                for h, v in enumerate(unpair(recvi, g, m)):
                    d_input[0, rows_of(g + 4 * h), cols] = v.astype(BF)

    swap_df.wait_recv()
    final = x_sum(zl) + dfq[...].astype(F32)
    for a in range(4):
        turned = final[:, a].reshape(64, 128).T
        d_filter[:, 128 * a:128 * a + 64] = turned[0:64]
        d_filter[:, 128 * a + 64:128 * a + 128] = turned[64:128]

    pltpu.make_async_copy(docs_all.at[0:31], docs_all.at[0:31], doc_s).wait()
    pltpu.make_async_copy(hall.at[0, 0:31], hall.at[0, 0:31], tap_s).wait()
    pltpu.make_async_copy(hall.at[0:3], hall.at[0:3], gat_s).wait()
    for ch, (start, stop) in enumerate(((0, 1), (1, 4))):
        part = sendu.at[start:stop, 0:31]
        pltpu.make_async_copy(part, part, u_s.at[ch]).wait()
    for ch in range(CI):
        await_all(sendd, ch, CI, d_s)
    for ch in range(CO):
        await_all(sendz, ch, CO, z_s)
        await_all(sendi, ch, CO, i_s)
    pltpu.make_async_copy(dfs.at[0:3], dfs.at[0:3], df_s).wait()
    swap_df.wait_send()


def local(grad_out, saved_input, gate_value, filter_taps, skip_gain, lang_ids, doc_ids, dro_weight):
    vmem = pl.BlockSpec(memory_space=pltpu.VMEM)
    dma = pltpu.SemaphoreType.DMA
    token = jax.ShapeDtypeStruct((1, 128, 2048), BF)
    return pl.pallas_call(
        kernel,
        out_shape=(token, token, jax.ShapeDtypeStruct((64, 512), F32)),
        in_specs=[pl.BlockSpec(memory_space=pl.ANY)] * 4 + [vmem] * 3 + [pl.BlockSpec(memory_space=pltpu.SMEM)] + [vmem] * 6,
        out_specs=(vmem, vmem, vmem),
        scratch_shapes=[
            *[pltpu.VMEM((1, 128, 2048), BF)] * 3,
            dma((3,)),
            pltpu.VMEM((1, 128), jnp.int32),
            pltpu.VMEM((NCTX, 1, 128), jnp.int32),
            pltpu.VMEM((NX, NCTX, 16, 128), BF),
            pltpu.VMEM((4, NCTX, 16, 128), BF),
            pltpu.VMEM((128, 128), F32),
            pltpu.VMEM((32, 256, 256), BF),
            pltpu.VMEM((32, 256, 256), BF),
            pltpu.VMEM((1024, 512), BF),
            pltpu.VMEM((512, 1024), BF),
            *[pltpu.VMEM((4, NCTX, 16, 128), BF)] * 8,
            pltpu.VMEM((32, 2, GR, 16, 128), BF),
            pltpu.VMEM((4, 32, 2, 16, 128), BF),
            pltpu.VMEM((4, 32, 2, 16, 128), BF),
            pltpu.VMEM((32, 256, 128), F32),
            pltpu.VMEM((32, 256, 128), F32),
            pltpu.VMEM((32, 256, 128), F32),
            pltpu.VMEM((NX, 2, 4, 4, 16, 128), BF),
            pltpu.VMEM((NX, 2, 4, 4, 16, 128), BF),
            pltpu.VMEM((4, 4, 16, 128), BF),
            pltpu.VMEM((4, 4, 16, 128), BF),
            dma, dma, dma, dma, dma, dma,
            *[dma((CI,))] * 4,
            *[dma((CO,))] * 4,
            dma, dma, dma, dma, dma((5,)),
        ],
        compiler_params=pltpu.CompilerParams(
            collective_id=0, has_side_effects=True, vmem_limit_bytes=60 << 20
        ),
        name="hyena_backward",
    )(
        grad_out, saved_input, gate_value, filter_taps, skip_gain.reshape(16, 128), lang_ids, doc_ids, dro_weight,
        *tables(),
    )


def solution(mesh):
    return jax.shard_map(
        local,
        mesh=mesh,
        in_specs=(
            P("dp", "ctx", None), P("dp", "ctx", None), P("dp", "ctx", None), P(None, "ctx"),
            P(), P("dp", "ctx"), P("dp", "ctx"), P(),
        ),
        out_specs=(P("dp", "ctx", None), P("dp", "ctx", None), P("ctx", "dp")),
        check_vma=False,
    )
```

```python
import functools
import math

import jax
import jax.numpy as jnp
import numpy as np
from jax import lax
from jax.experimental import pallas as pl
from jax.experimental.pallas import tpu as pltpu
from jax.sharding import PartitionSpec as P

MESH = pl.DeviceIdType.MESH
BF = jnp.bfloat16
F32 = jnp.float32
NCTX, NDP, NX = 32, 8, 4
LEN = 4096
CC = (2, 2)
FIRST = 1
GR = 8
CI, CO = CC
UN = 8
US = 31
BACK = ((0, 1), (1, 4))


def tables():
    k1 = np.arange(32)
    a = np.arange(32)
    b = np.arange(128)
    phi = 2 * math.pi / 128 * ((a[None, :] * (4 * k1[:, None] + 1)) % 128)
    first = np.zeros((64, 128), np.float32)
    first[:, :32] = np.stack([np.cos(phi), -np.sin(phi)], 1).reshape(64, 32)
    last = np.zeros((32, 128), np.float32)
    last[:, :64] = first[:, :32].T / LEN
    alpha = 2 * math.pi / 16384 * ((b[None, :] * (4 * k1[:, None] + 1)) % 16384)
    beta = 2 * math.pi / 128 * ((b[None, :] * b[:, None]) % 128)
    f = lambda v: jnp.asarray(v.astype(np.float32))
    return (
        jnp.asarray(first, BF),
        jnp.asarray(last, BF),
        f(np.cos(alpha)),
        f(np.sin(alpha)),
        f(np.cos(beta)),
        f(np.sin(beta)),
    )


def iota(shape, dim):
    return lax.broadcasted_iota(jnp.int32, shape, dim)


def swap(x):
    return pltpu.roll(x, 64, axis=1)


def kernel(
    grad_hbm, sig_hbm, gate_hbm, taps, skip, lang, docs, dro, first, last, cosa, sina, cosb, sinb,
    d_input, d_gate, d_filter,
    grad, sig, gate, stage, docs_out, docs_all, hall, htime, scale, mats, matst, fone, ftwo, sendu, recvu, sendd, recvd, sendz, recvz,
    sendi, recvi, ybuf, vbuf, qbuf, hspec, uspec, gspec, dfs, dfr, dft, dfq,
    doc_s, doc_r, tap_s, tap_r, gat_s, gat_r, u_s, u_r, d_s, d_r, z_s, z_r, i_s, i_r, df_s, df_r, dq_s, dq_r, own,
):
    me = lax.axis_index("ctx")
    dp = lax.axis_index("dp")
    xs = lax.rem(dp, NX)
    zl = dp // NX
    low = iota((16, 128), 1) < 64

    def peer_of(p):
        return lax.rem(me + p, NCTX)

    def x_of(q):
        return zl * NX + lax.rem(xs + q, NX)

    staged = [
        pltpu.make_async_copy(src, dst, stage.at[i])
        for i, (src, dst) in enumerate(((sig_hbm, sig), (grad_hbm, grad), (gate_hbm, gate)))
    ]
    for copy in staged:
        copy.start()
    barrier = pltpu.get_barrier_semaphore()

    @pl.loop(1, NCTX)
    def _(p):
        pl.semaphore_signal(barrier, inc=1, device_id={"ctx": peer_of(p)}, device_id_type=MESH)

    across = lax.rem(dp + NX, NDP)

    @pl.loop(1, NX)
    def _(q):
        pl.semaphore_signal(barrier, inc=1, device_id={"dp": x_of(q)}, device_id_type=MESH)

    pl.semaphore_signal(barrier, inc=1, device_id={"dp": across}, device_id_type=MESH)

    def pair_store(dst, g, m, first_half, second_half):
        dst[g, 2 * m] = jnp.where(low, first_half, swap(second_half)).astype(BF)
        dst[g, 2 * m + 1] = jnp.where(low, swap(first_half), second_half).astype(BF)

    def rows_of(g):
        return pl.ds(pl.multiple_of(16 * g, 16), 16)

    docs_row = docs[...]
    docs_out[...] = docs_row
    docs_all[me] = docs_row

    pl.semaphore_wait(barrier, NCTX - 1 + NX)

    @pl.loop(1, NCTX)
    def _(p):
        peer = peer_of(p)
        pltpu.make_async_remote_copy(
            docs_out, docs_all.at[me], doc_s, doc_r, device_id={"ctx": peer}, device_id_type=MESH
        ).start()

    def tap_rows(j):
        return taps.at[pl.ds(pl.multiple_of(64 * j + 16 * xs, 16), 16), :]

    @pl.loop(1, NCTX)
    def _(p):
        peer = peer_of(p)
        pltpu.make_async_remote_copy(
            tap_rows(peer), hall.at[xs, me], tap_s, tap_r, device_id={"ctx": peer}, device_id_type=MESH
        ).start()

    own_taps = pltpu.make_async_copy(tap_rows(me), hall.at[xs, me], own.at[0])
    own_taps.start()

    def send_part(src, dst, span, sems, semr):
        @pl.loop(1, NCTX, unroll=US)
        def _(p):
            peer = peer_of(p)
            pltpu.make_async_remote_copy(
                src.at[span, peer], dst.at[span, me], sems, semr,
                device_id={"ctx": peer}, device_id_type=MESH,
            ).start()

    def spread(src, dst, chunk, chunks, sems, semr):
        per = src.shape[0] // chunks
        send_part(src, dst, slice(per * chunk, per * chunk + per), sems.at[chunk], semr.at[chunk])

    def await_all(buf, chunk, chunks, sem):
        per = buf.shape[0] // chunks
        part = buf.at[per * chunk:per * chunk + per, 0:31]
        pltpu.make_async_copy(part, part, sem.at[chunk]).wait()

    staged[0].wait()

    @pl.loop(0, 4)
    def _(g):
        for m in range(16):
            cols = slice(128 * m, 128 * m + 128)
            pair_store(sendu, g, m, sig[0, rows_of(g), cols].astype(F32), sig[0, rows_of(g + 4), cols].astype(F32))

    send_part(sendu, recvu, slice(0, 1), u_s.at[0], u_r.at[0])

    own_taps.wait()
    pltpu.make_async_copy(hall.at[0, 0:31], hall.at[0, 0:31], tap_r).wait()

    @pl.loop(1, NX)
    def _(q):
        pltpu.make_async_remote_copy(
            hall.at[xs], hall.at[xs], gat_s, gat_r, device_id={"dp": x_of(q)}, device_id_type=MESH
        ).start()

    send_part(sendu, recvu, slice(1, 4), u_s.at[1], u_r.at[1])

    staged[1].wait()
    staged[2].wait()

    def column(row):
        return jnp.broadcast_to(row.astype(F32), (128, 128)).T

    own_docs = column(docs_row)
    own_lang = column(lang[...])
    weight = jnp.zeros((128, 128), F32)
    for group in range(16):
        weight = jnp.where(own_lang == float(group), dro[group], weight)
    pltpu.make_async_copy(docs_all.at[0:31], docs_all.at[0:31], doc_r).wait()

    def count(a, total):
        row = jnp.broadcast_to(docs_all[a].astype(F32), (128, 128))
        return total + jnp.where(row == own_docs, 1.0, 0.0)

    hits = lax.fori_loop(0, NCTX, count, jnp.zeros((128, 128), F32))
    doc_len = jnp.sum(hits, axis=1, keepdims=True)
    scale[...] = weight * 256.0 / (doc_len + 128.0)

    for ch in range(CI):
        @pl.loop(4 // CI * ch, 4 // CI * ch + 4 // CI)
        def _(g):
            for m in range(16):
                cols = slice(128 * m, 128 * m + 128)
                halves = []
                for h in range(2):
                    rows = rows_of(g + 4 * h)
                    dy = grad[0, rows, cols].astype(F32) * scale[rows, :]
                    halves.append(dy * gate[0, rows, cols].astype(F32))
                pair_store(sendd, g, m, *halves)

        spread(sendd, recvd, ch, CI, d_s, d_r)

    own_u = pltpu.make_async_copy(sendu.at[:, me], recvu.at[:, me], own.at[1])
    own_u.start()
    own_d = pltpu.make_async_copy(sendd.at[:, me], recvd.at[:, me], own.at[4])
    own_d.start()

    def expand(small, rows, cols):
        left = (iota((rows, small.shape[0]), 0) // 16 == iota((rows, small.shape[0]), 1)).astype(F32).astype(BF)
        right = (iota((128, cols), 1) // 16 == iota((128, cols), 0)).astype(F32).astype(BF)
        tall = jnp.dot(left, small, preferred_element_type=F32).astype(BF)
        wide = jnp.dot(tall, right, preferred_element_type=F32)
        keep = lax.rem(iota((rows, cols), 0), 16) == lax.rem(iota((rows, cols), 1), 16)
        return jnp.where(keep, wide, 0.0).astype(BF)

    fone[...] = expand(first[...], 1024, 512)
    ftwo[...] = expand(last[...], 512, 1024)

    @pl.loop(0, 32, unroll=2)
    def _(k):
        ca, sa = cosa[pl.ds(k, 1), :], sina[pl.ds(k, 1), :]
        co = ca * cosb[...] - sa * sinb[...]
        si = sa * cosb[...] + ca * sinb[...]
        mats[k, 0:128, 0:128] = co.astype(BF)
        mats[k, 0:128, 128:256] = si.astype(BF)
        mats[k, 128:256, 0:128] = (-si).astype(BF)
        mats[k, 128:256, 128:256] = co.astype(BF)
        cot, sit = co.T, si.T
        matst[k, 0:128, 0:128] = cot.astype(BF)
        matst[k, 0:128, 128:256] = (-sit).astype(BF)
        matst[k, 128:256, 0:128] = sit.astype(BF)
        matst[k, 128:256, 128:256] = cot.astype(BF)

    def stage_one(x, g, lanes):
        y = jnp.dot(fone[...], x.reshape(512, 128), preferred_element_type=F32)
        ybuf[:, :, g, :, 0:lanes] = y[:, 0:lanes].astype(BF).reshape(32, 2, 16, lanes)
        ybuf[:, :, g + 4, :, 0:lanes] = swap(y)[:, 0:lanes].astype(BF).reshape(32, 2, 16, lanes)

    def stage_two(k):
        return jnp.dot(mats[k], ybuf[k].reshape(256, 128), preferred_element_type=F32)

    pltpu.make_async_copy(hall.at[0:3], hall.at[0:3], gat_r).wait()

    @pl.loop(0, NCTX, unroll=4)
    def _(a):
        block = hall[:, a].reshape(64, 128).astype(F32)
        turned = jnp.concatenate([swap(block), block], axis=0).T
        htime[:, a] = turned[0:64].astype(BF).reshape(4, 16, 128)

    @pl.loop(0, 4)
    def _(g):
        stage_one(htime[g], g, 128)

    gain = skip[pl.ds(me // 2, 1), :]
    turned_gain = pltpu.roll(jnp.broadcast_to(gain, (8, 128)), 64, axis=1)[0:1]
    low_row = iota((1, 128), 1) < 64
    even = jnp.where(low_row, gain, turned_gain)
    odd = jnp.where(low_row, turned_gain, gain)
    parity = lax.rem(me, 2).astype(F32)
    gain2 = even * (1.0 - parity) + odd * parity
    half_low = iota((64, 128), 1) < 64

    def invert(k, p, buf):
        v = jnp.dot(matst[k], p.astype(BF), preferred_element_type=F32).reshape(2, 2, 64, 128)
        for c in range(2):
            both = jnp.where(half_low, v[c, 0], swap(v[c, 1]))
            buf[:, k, c] = both.astype(BF).reshape(4, 16, 128)

    def bring(recv, local_copy, sem, spans):
        local_copy.wait()
        for ch, (start, stop) in enumerate(spans):
            part = recv.at[start:stop, 0:31]
            pltpu.make_async_copy(part, part, sem.at[ch]).wait()

            @pl.loop(start, stop)
            def _(g):
                stage_one(recv[g], g, 64)

    def send_back(source, send, recv, chunks, sems, semr):
        for ch in chunks:
            start, stop = BACK[ch]

            @pl.loop(start, stop)
            def _(g):
                o = jnp.dot(ftwo[...], vbuf[g].reshape(1024, 128), preferred_element_type=F32)
                o = o + gain2 * source[g].reshape(512, 128).astype(F32)
                send[g] = o.astype(BF).reshape(32, 16, 128)

            send_part(send, recv, slice(start, stop), sems.at[ch], semr.at[ch])

    bring(recvu, own_u, u_r, ((0, 1), (1, 4)))

    @pl.loop(0, 32, unroll=UN)
    def _(k):
        s = stage_two(k)
        uspec[k] = s
        h = swap(s)
        hspec[k] = h
        sr, si = s[0:128], s[128:256]
        hr, hi = h[0:128], h[128:256]
        invert(k, jnp.concatenate([sr * hr - si * hi, sr * hi + si * hr], axis=0), vbuf)

    send_back(recvu, sendz, recvz, range(CO), z_s, z_r)
    own_z = pltpu.make_async_copy(sendz.at[:, me], recvz.at[:, me], own.at[2])
    own_z.start()

    bring(recvd, own_d, d_r, ((0, 2), (2, 4)))

    @pl.loop(0, 32, unroll=UN)
    def _(k):
        s = stage_two(k)
        gspec[k] = s
        sr, si = s[0:128], s[128:256]
        hr, hi = hspec[k, 0:128], hspec[k, 128:256]
        invert(k, jnp.concatenate([sr * hr + si * hi, si * hr - sr * hi], axis=0), vbuf)

    send_back(recvd, sendi, recvi, range(FIRST), i_s, i_r)

    @pl.loop(0, 32, unroll=UN)
    def _(k):
        sr, si = gspec[k, 0:128], gspec[k, 128:256]
        ur, ui = uspec[k, 0:128], uspec[k, 128:256]
        invert(k, jnp.concatenate([sr * ur + si * ui, si * ur - sr * ui], axis=0), qbuf)

    @pl.loop(0, 4)
    def _(g):
        o = jnp.dot(ftwo[...], qbuf[g].reshape(1024, 128), preferred_element_type=F32)
        o = o.astype(BF).reshape(2, 4, 4, 16, 128)
        dfs[:, 0, g] = o[0]
        dfs[:, 1, g] = o[1]

    @pl.loop(1, NX)
    def _(q):
        other = lax.rem(xs + q, NX)
        pltpu.make_async_remote_copy(
            dfs.at[other], dfr.at[xs], df_s, df_r, device_id={"dp": x_of(q)}, device_id_type=MESH
        ).start()

    own_df = pltpu.make_async_copy(dfs.at[xs], dfr.at[xs], own.at[3])
    own_df.start()
    send_back(recvd, sendi, recvi, range(FIRST, CO), i_s, i_r)
    own_i = pltpu.make_async_copy(sendi.at[:, me], recvi.at[:, me], own.at[0])
    own_i.start()

    own_df.wait()
    pltpu.make_async_copy(dfr.at[0:3], dfr.at[0:3], df_r).wait()

    def x_sum(zside):
        total = dfr[0, zside].astype(F32)
        for r in range(1, NX):
            total = total + dfr[r, zside].astype(F32)
        return total

    dft[...] = x_sum(1 - zl).astype(BF)
    swap_df = pltpu.make_async_remote_copy(
        dft, dfq, dq_s, dq_r, device_id={"dp": across}, device_id_type=MESH
    )
    swap_df.start()
    own_z.wait()
    own_i.wait()

    def unpair(recv, g, m):
        left, right = recv[g, 2 * m].astype(F32), recv[g, 2 * m + 1].astype(F32)
        return jnp.where(low, left, swap(right)), jnp.where(low, swap(left), right)

    def await_span(buf, ch, sem):
        start, stop = BACK[ch]
        part = buf.at[start:stop, 0:31]
        pltpu.make_async_copy(part, part, sem.at[ch]).wait()

    for ch in range(CO):
        await_span(recvz, ch, z_r)

        @pl.loop(*BACK[ch])
        def _(g):
            for m in range(16):
                cols = slice(128 * m, 128 * m + 128)
                for h, z in enumerate(unpair(recvz, g, m)):
                    rows = rows_of(g + 4 * h)
                    d_gate[0, rows, cols] = (grad[0, rows, cols].astype(F32) * scale[rows, :] * z).astype(BF)

    for ch in range(CO):
        await_span(recvi, ch, i_r)

        @pl.loop(*BACK[ch])
        def _(g):
            for m in range(16):
                cols = slice(128 * m, 128 * m + 128)
                for h, v in enumerate(unpair(recvi, g, m)):
                    d_input[0, rows_of(g + 4 * h), cols] = v.astype(BF)

    swap_df.wait_recv()
    final = x_sum(zl) + dfq[...].astype(F32)
    for a in range(4):
        turned = final[:, a].reshape(64, 128).T
        d_filter[:, 128 * a:128 * a + 64] = turned[0:64]
        d_filter[:, 128 * a + 64:128 * a + 128] = turned[64:128]

    pltpu.make_async_copy(docs_all.at[0:31], docs_all.at[0:31], doc_s).wait()
    pltpu.make_async_copy(hall.at[0, 0:31], hall.at[0, 0:31], tap_s).wait()
    pltpu.make_async_copy(hall.at[0:3], hall.at[0:3], gat_s).wait()
    for ch, (start, stop) in enumerate(((0, 1), (1, 4))):
        part = sendu.at[start:stop, 0:31]
        pltpu.make_async_copy(part, part, u_s.at[ch]).wait()
    for ch in range(CI):
        await_all(sendd, ch, CI, d_s)
    for ch in range(CO):
        await_span(sendz, ch, z_s)
        await_span(sendi, ch, i_s)
    pltpu.make_async_copy(dfs.at[0:3], dfs.at[0:3], df_s).wait()
    swap_df.wait_send()


def local(grad_out, saved_input, gate_value, filter_taps, skip_gain, lang_ids, doc_ids, dro_weight):
    vmem = pl.BlockSpec(memory_space=pltpu.VMEM)
    dma = pltpu.SemaphoreType.DMA
    token = jax.ShapeDtypeStruct((1, 128, 2048), BF)
    return pl.pallas_call(
        kernel,
        out_shape=(token, token, jax.ShapeDtypeStruct((64, 512), F32)),
        in_specs=[pl.BlockSpec(memory_space=pl.ANY)] * 4 + [vmem] * 3 + [pl.BlockSpec(memory_space=pltpu.SMEM)] + [vmem] * 6,
        out_specs=(vmem, vmem, vmem),
        scratch_shapes=[
            *[pltpu.VMEM((1, 128, 2048), BF)] * 3,
            dma((3,)),
            pltpu.VMEM((1, 128), jnp.int32),
            pltpu.VMEM((NCTX, 1, 128), jnp.int32),
            pltpu.VMEM((NX, NCTX, 16, 128), BF),
            pltpu.VMEM((4, NCTX, 16, 128), BF),
            pltpu.VMEM((128, 128), F32),
            pltpu.VMEM((32, 256, 256), BF),
            pltpu.VMEM((32, 256, 256), BF),
            pltpu.VMEM((1024, 512), BF),
            pltpu.VMEM((512, 1024), BF),
            *[pltpu.VMEM((4, NCTX, 16, 128), BF)] * 8,
            pltpu.VMEM((32, 2, GR, 16, 128), BF),
            pltpu.VMEM((4, 32, 2, 16, 128), BF),
            pltpu.VMEM((4, 32, 2, 16, 128), BF),
            pltpu.VMEM((32, 256, 128), F32),
            pltpu.VMEM((32, 256, 128), F32),
            pltpu.VMEM((32, 256, 128), F32),
            pltpu.VMEM((NX, 2, 4, 4, 16, 128), BF),
            pltpu.VMEM((NX, 2, 4, 4, 16, 128), BF),
            pltpu.VMEM((4, 4, 16, 128), BF),
            pltpu.VMEM((4, 4, 16, 128), BF),
            dma, dma, dma, dma, dma, dma,
            *[dma((CI,))] * 4,
            *[dma((CO,))] * 4,
            dma, dma, dma, dma, dma((5,)),
        ],
        compiler_params=pltpu.CompilerParams(
            collective_id=0, has_side_effects=True, vmem_limit_bytes=60 << 20
        ),
        name="hyena_backward",
    )(
        grad_out, saved_input, gate_value, filter_taps, skip_gain.reshape(16, 128), lang_ids, doc_ids, dro_weight,
        *tables(),
    )


def solution(mesh):
    return jax.shard_map(
        local,
        mesh=mesh,
        in_specs=(
            P("dp", "ctx", None), P("dp", "ctx", None), P("dp", "ctx", None), P(None, "ctx"),
            P(), P("dp", "ctx"), P("dp", "ctx"), P(),
        ),
        out_specs=(P("dp", "ctx", None), P("dp", "ctx", None), P("ctx", "dp")),
        check_vma=False,
    )
```
